512 devices in a mesh: expert: 64 (over z, y), replica: 8 (over x, core).
Axes of the slice: x: 4, y: 4, z: 16, core: 2. Of those that a mesh axis runs over, the one named last changes fastest.
Arguments:
- cotangent: bfloat16 [65536, 2048], P(('expert', 'replica')), may hold values from -2 to 2
- hidden: bfloat16 [65536, 6, 704], P(('expert', 'replica')), may hold values from -24 to 24
- routes: int32 [65536, 6], P(('expert', 'replica')), may hold values from 0 to 63, all different within a row; in each aligned block of 128 rows (0 to 127, 128 to 255, ...) at most 18 rows name the same one
- numerators: int32 [65536, 6], P(('expert', 'replica')), may hold values from 1 to 1024
- w_down: bfloat16 [64, 704, 2048], P('expert'), may hold values from -0.21875 to 0.21875
Outputs:
- gate_grad: float32 [65536, 6], P(('expert', 'replica'))
- grad_scales: float32 [64, 704, 16], P('expert', 'replica')
- grad_mantissa: float32 [64, 704, 2048], P('expert', 'replica')
The draws below stay inside these ranges and needn't reach their ends.
Inputs may be any that keep to these rules, and one draw needn't show every extreme that they name: `routes`: no expert is named by more than 18 rows of one device's tokens, a bound that some blocks reach.
All inputs are finite; a program needn't handle non-finite values. Where the reference program divides by a largest or mean magnitude, that divisor is 1e-20 or more.
Results may differ from the reference program's by a relative error of at most 0.023.
Values may be sent and summed in bfloat16 or wider, within the bound.
A program may use at most 64 MiB of HBM per device.

```python
import math
import jax
import jax.numpy as jnp
import numpy as np
from jax import lax

D = 2048
HID = 704
TOP = 6
BLOCK = 128
TOK_DEV = 128
E = 64
TOKENS = 65536
SLOTS = 18
N_EXPERT = 64
N_REPLICA = 8


def draw_cotangent(key, part):
    keys = jax.random.split(key, 3)
    row_scale = jnp.exp(jax.random.uniform(keys[1], (TOKENS, 1), jnp.float32) * math.log(10.0))
    col_scale = jnp.exp(jax.random.uniform(keys[2], (1, D), jnp.float32) * math.log(10.0))
    position = (jnp.arange(TOKENS) // TOK_DEV % N_REPLICA).astype(jnp.float32) / max(N_REPLICA - 1, 1)
    values = jnp.clip(jax.random.normal(keys[0], (TOKENS, D), jnp.float32), -5.0, 5.0)
    factor = jnp.power(3.0, position)
    return (0.0007 * values * row_scale * col_scale * factor[:, None]).astype(jnp.bfloat16)


def draw_hidden(key, part):
    keys = jax.random.split(key, 2)
    col_scale = jnp.exp(jax.random.uniform(keys[1], (1, 1, HID), jnp.float32) * math.log(10.0))
    values = jnp.clip(jax.random.normal(keys[0], (TOKENS, TOP, HID), jnp.float32), -6.0, 6.0)
    return (0.3 * values * col_scale).astype(jnp.bfloat16)


def touch_ends(drawn, stream_key, least, top_value):
    place = [jax.random.randint(jax.random.fold_in(stream_key, axis), (), 0, length) for axis, length in enumerate(drawn.shape)]
    widest = drawn.shape.index(max(drawn.shape))
    beside = place[:widest] + [(place[widest] + 1) % drawn.shape[widest]] + place[widest + 1:]
    return drawn.at[tuple(place)].set(least).at[tuple(beside)].set(top_value)


def levels(key, dims, shards, low, top_value):
    gain, own = 1.0, jax.random.fold_in(key, 6)
    for dim, parts in shards:
        heights = jnp.exp(jax.random.uniform(jax.random.fold_in(own, dim), (parts,), jnp.float32, low / len(shards), top_value / len(shards)))
        gain = gain * jnp.repeat(heights, dims[dim] // parts).reshape([-1 if axis == dim else 1 for axis in range(len(dims))])
    return gain


def routed_block(rng, own, number, rows, number_of, top, reach, lean):
    ranking = jax.random.permutation(rng, number_of)
    heavy_load, ordinary = load_shares(number_of, rows * top, reach, lean, True), load_shares(number_of, rows * top, reach, lean, False)
    places = jnp.arange(number_of)

    def named(lengths, offset_by):
        used = int((lengths > 0).sum())
        fixed = max(1, used // 4)
        passed = fixed + (places - fixed + offset_by * (used - fixed)) % max(1, number_of - fixed)
        return jnp.zeros((number_of,), jnp.int32).at[ranking[jnp.where(places < fixed, places, passed)]].set(jnp.asarray(lengths, jnp.int32))

    lengths = jnp.where(number % 4 == 0, named(heavy_load, number // 4), named(ordinary, number - number // 4 - 1))
    mixed = jax.random.permutation(jax.random.fold_in(own, 3), number_of)
    donor, receiver = mixed[0:number_of // 2 * 2:2], mixed[1:number_of // 2 * 2:2]
    margin = jnp.minimum(lengths[donor] - 1, reach - lengths[receiver]) // 2
    margin = jnp.where((donor == ranking[0]) | (receiver == ranking[0]) | (lengths[receiver] == 0), 0, jnp.maximum(margin, 0))
    passed = jax.random.randint(jax.random.fold_in(own, 4), (number_of // 2,), 0, 1 << 20) % (margin + 1)
    lengths = lengths.at[donor].add(-passed).at[receiver].add(passed)
    members = jnp.searchsorted(jnp.cumsum(lengths), jnp.arange(rows * top), side="right").astype(jnp.int32)
    table = members.reshape(top, rows).T
    table = table[jax.random.permutation(jax.random.fold_in(own, 1), rows)]
    offset_by = jax.random.randint(jax.random.fold_in(own, 2), (rows, 1), 0, top)
    return jnp.take_along_axis(table, (jnp.arange(top)[None, :] + offset_by) % top, axis=1)


def load_shares(amount, total, reach, lean, full):
    portions = [(1 << 20) // math.isqrt(standing ** lean) + 1 for standing in range(1, amount + 1)]
    largest = reach if full else min(reach, max(-(-total // amount), total * portions[0] // sum(portions)))
    least = 1 if total - largest >= amount - 1 else 0
    holding, rest = [largest] + [least] * (amount - 1), total - largest - least * (amount - 1)
    while rest > 0:
        candidates = [i for i in range(1, amount) if holding[i] < largest] or [i for i in range(1, amount) if holding[i] < reach]
        whole, left = sum([portions[i] for i in candidates]), rest
        for i in candidates:
            extra = min(reach - holding[i], max(1, left * portions[i] // whole), rest)
            holding[i] = holding[i] + extra
            rest = rest - extra
    return np.array(holding)


def noise(rng, dims, width, bound, cuts=(), kind=jnp.bfloat16):
    gain = levels(rng, dims, cuts, -0.22, 0.18) if cuts else 1.0
    drawn = jax.random.normal(rng, dims, jnp.float32) * width * gain
    return jnp.minimum(jnp.maximum(drawn, -bound), bound).astype(kind)


def setup_inputs(seed: int = 0) -> dict:
    key_list = jax.random.split(jax.random.key(seed), 6)
    cotangent = draw_cotangent(jax.random.fold_in(key_list[5], 71), 0)
    hidden = draw_hidden(jax.random.fold_in(key_list[5], 71), 0)
    routes_keys = jax.random.split(jax.random.fold_in(key_list[2], 1), TOKENS // TOK_DEV)
    routes_turns = jax.random.permutation(jax.random.fold_in(key_list[2], 3), TOKENS // TOK_DEV)
    routes = jax.vmap(lambda own, number: routed_block(jax.random.fold_in(key_list[2], 2), own, number, TOK_DEV, E, TOP, SLOTS, 2))(routes_keys, routes_turns).reshape((TOKENS, TOP))
    numerators = touch_ends(jax.random.randint(key_list[3], (TOKENS, TOP), 1, 1025), jax.random.fold_in(key_list[3], 1), 1, 1024).astype(jnp.int32)
    w_down = noise(key_list[4], (E, HID, D), HID ** -0.5, 0.21875, ((0, 64),))
    return dict(cotangent=cotangent, hidden=hidden, routes=routes, numerators=numerators, w_down=w_down)


def pair_terms(cot_group, hid_group, route_group, weight_group, matrix, expert_id):
    routed = TOK_DEV * TOP
    chosen = (route_group == expert_id).astype(jnp.int32)
    before = jnp.cumsum(chosen, axis=1).astype(jnp.int32) - chosen
    target = jnp.where(chosen > 0, before, SLOTS).astype(jnp.int32)
    sources = jnp.broadcast_to(jnp.arange(N_EXPERT, dtype=jnp.int32)[:, None], (N_EXPERT, routed))
    row_ids = jnp.broadcast_to(jnp.arange(routed, dtype=jnp.int32)[None, :], (N_EXPERT, routed))
    slot_table = jnp.full((N_EXPERT, SLOTS + 1), routed, jnp.int32).at[sources, target].set(row_ids)
    slot_table = slot_table[:, :SLOTS]
    in_use = slot_table < routed
    clipped = jnp.minimum(slot_table, routed - 1).astype(jnp.int32)
    hid_sel = jnp.take_along_axis(hid_group, clipped[:, :, None], axis=1)
    hid_sel = jnp.where(in_use[:, :, None], hid_sel, jnp.zeros_like(hid_sel))
    cot_sel = jnp.take_along_axis(cot_group, (clipped // TOP).astype(jnp.int32)[:, :, None], axis=1)
    cot_sel = jnp.where(in_use[:, :, None], cot_sel, jnp.zeros_like(cot_sel))
    weight_sel = jnp.where(in_use, jnp.take_along_axis(weight_group, clipped, axis=1), jnp.float32(0.0))
    cot_flat = cot_sel.reshape(N_EXPERT * SLOTS, D)
    hid_flat = hid_sel.reshape(N_EXPERT * SLOTS, HID)
    back_proj = jnp.dot(cot_flat, matrix.T, preferred_element_type=jnp.float32)
    gate_vals = jnp.sum(back_proj * hid_flat.astype(jnp.float32), axis=1).reshape(N_EXPERT, SLOTS)
    scaled = (weight_sel.reshape(N_EXPERT * SLOTS)[:, None] * cot_flat.astype(jnp.float32)).astype(jnp.bfloat16)
    partial_value = jnp.dot(hid_flat.T, scaled, preferred_element_type=jnp.float32)
    slot_sources = jnp.broadcast_to(jnp.arange(N_EXPERT, dtype=jnp.int32)[:, None], (N_EXPERT, SLOTS))
    spread = jnp.zeros((N_EXPERT, routed + 1), jnp.float32).at[slot_sources, slot_table].set(
        jnp.where(in_use, gate_vals, jnp.float32(0.0)))
    return partial_value, spread[:, :routed]


def reference(cotangent, hidden, routes, numerators, w_down):
    routed = TOK_DEV * TOP
    cot_all = cotangent.reshape(N_EXPERT, N_REPLICA, TOK_DEV, D)
    hid_all = hidden.reshape(N_EXPERT, N_REPLICA, routed, HID)
    route_all = routes.reshape(N_EXPERT, N_REPLICA, routed)
    weight_all = numerators.reshape(N_EXPERT, N_REPLICA, routed).astype(jnp.float32) / 1024.0

    def per_expert(gate_acc, expert_id):
        matrix = w_down[expert_id]

        def per_replica(group_id):
            return pair_terms(cot_all[:, group_id], hid_all[:, group_id], route_all[:, group_id],
                              weight_all[:, group_id], matrix, expert_id)

        partials, spreads = lax.map(per_replica, jnp.arange(N_REPLICA, dtype=jnp.int32))
        blocks = partials.reshape(N_REPLICA, HID, D // BLOCK, BLOCK)
        scales = jnp.max(jnp.max(jnp.abs(blocks), axis=3), axis=0) + 1e-6
        mantissa = (blocks / scales[None, :, :, None]).astype(jnp.bfloat16)
        mantissa = lax.optimization_barrier(mantissa).astype(jnp.float32)
        summed = jnp.sum(mantissa, axis=0).reshape(HID, D)
        return gate_acc + jnp.transpose(spreads, (1, 0, 2)), (scales, summed)

    start_acc = jnp.zeros((N_EXPERT, N_REPLICA, routed), jnp.float32)
    gate_acc, outputs = lax.scan(per_expert, start_acc, jnp.arange(E, dtype=jnp.int32))
    gate_grad = gate_acc.reshape(N_EXPERT * N_REPLICA * TOK_DEV, TOP)
    return gate_grad, outputs[0], outputs[1]
```

```python
import jax
import jax.numpy as jnp
from jax import lax
from jax.sharding import Mesh, PartitionSpec as P

BLOCK = 128
NZ, NY, NX, NC = 16, 4, 4, 2
SLOTS = 18
COLS = 768


def per_device(cotangent, hidden, routes, numerators, w_down):
    tok, width = cotangent.shape
    top, hid = hidden.shape[1], hidden.shape[2]
    routed = tok * top
    experts = NZ * NY
    flat = routes.reshape(routed)
    one_hot = flat[:, None] == jnp.arange(experts, dtype=jnp.int32)[None, :]
    one_hot_b = one_hot.astype(jnp.bfloat16)
    row = jnp.arange(routed, dtype=jnp.int32)
    lower = (row[:, None] > row[None, :]).astype(jnp.bfloat16)
    before = jnp.dot(lower, one_hot_b, preferred_element_type=jnp.float32)
    rank = jnp.sum(jnp.where(one_hot, before, 0.0), axis=1).astype(jnp.int32)
    slot = flat * SLOTS + rank
    pack = (jnp.arange(experts * SLOTS, dtype=jnp.int32)[:, None] == slot[None, :]).astype(
        jnp.bfloat16
    )
    flat_n = numerators.reshape(routed)
    extra = jnp.concatenate(
        [
            (flat_n // 32).astype(jnp.bfloat16)[:, None],
            (flat_n % 32).astype(jnp.bfloat16)[:, None],
            jnp.zeros((routed, COLS - hid - 2), jnp.bfloat16),
        ],
        axis=1,
    )
    rows = jnp.concatenate([hidden.reshape(routed, hid), extra], axis=1)
    packed = jnp.dot(pack, rows, preferred_element_type=jnp.float32).astype(jnp.bfloat16)
    held = jnp.max(
        jnp.where(one_hot, rank[:, None] + 1, 0).reshape(tok, top, experts), axis=1
    )
    table = (held - 1).T.astype(jnp.float32).reshape(NZ, NY, tok)

    cots = lax.all_gather(cotangent, "z")
    ranks = lax.all_to_all(table, "z", split_axis=0, concat_axis=0, tiled=True)
    hid_z = lax.all_to_all(
        packed.reshape(NZ, NY * SLOTS, COLS), "z", split_axis=0, concat_axis=0, tiled=True
    )
    hid_y = hid_z.reshape(NZ, NY, SLOTS, COLS).transpose(1, 0, 2, 3)
    got_hid = lax.all_to_all(
        hid_y.reshape(NY, NZ * SLOTS, COLS), "y", split_axis=0, concat_axis=0, tiled=True
    ).reshape(experts * SLOTS, COLS)
    select = (
        ranks[:, :, None, :] == jnp.arange(SLOTS, dtype=jnp.float32)[None, None, :, None]
    ).astype(jnp.bfloat16)
    picked = lax.dot_general(
        select.reshape(NZ, NY * SLOTS, tok),
        cots,
        (((2,), (1,)), ((0,), (0,))),
        preferred_element_type=jnp.float32,
    ).astype(jnp.bfloat16)
    cot_y = picked.reshape(NZ, NY, SLOTS, width).transpose(1, 0, 2, 3)
    cot_rows = lax.all_to_all(
        cot_y.reshape(NY, NZ * SLOTS, width), "y", split_axis=0, concat_axis=0, tiled=True
    ).reshape(experts * SLOTS, width)

    hid_rows = got_hid[:, :hid]
    weight = (
        got_hid[:, hid].astype(jnp.float32) * 32.0 + got_hid[:, hid + 1].astype(jnp.float32)
    ) / 1024.0
    back = lax.dot_general(
        cot_rows, w_down[0], (((1,), (1,)), ((), ())), preferred_element_type=jnp.float32
    )
    gate = jnp.sum(back * hid_rows.astype(jnp.float32), axis=1)
    gate_y = lax.all_to_all(
        gate.reshape(NY, NZ * SLOTS), "y", split_axis=0, concat_axis=0, tiled=True
    )
    gate_z = lax.all_to_all(
        gate_y.reshape(NY, NZ, SLOTS).transpose(1, 0, 2).reshape(NZ, NY * SLOTS),
        "z",
        split_axis=0,
        concat_axis=0,
        tiled=True,
    )
    gate_grad = jnp.sum(
        jnp.where(pack > 0, gate_z.reshape(experts * SLOTS)[:, None], 0.0), axis=0
    ).reshape(tok, top)

    weighted = (hid_rows.astype(jnp.float32) * weight[:, None]).astype(jnp.bfloat16)
    partial_value = lax.dot_general(
        weighted, cot_rows, (((0,), (0,)), ((), ())), preferred_element_type=jnp.float32
    ).astype(jnp.bfloat16)
    replicas = NX * NC
    share = hid // replicas
    parts = lax.all_to_all(
        partial_value.reshape(replicas, share, width),
        ("x", "c"),
        split_axis=0,
        concat_axis=0,
        tiled=True,
    ).astype(jnp.float32)
    blocks = parts.reshape(replicas, share, width // BLOCK, BLOCK)
    scales = jnp.max(jnp.max(jnp.abs(blocks), axis=3), axis=0) + 1e-6
    total = jnp.sum(blocks, axis=0) / scales[:, :, None]
    return gate_grad, scales[None], total.reshape(1, share, width)


def solution(mesh):
    fine = Mesh(mesh.devices.reshape(NZ, NY, NX, NC), ("z", "y", "x", "c"))
    every = ("z", "y", "x", "c")
    expert, replica = ("z", "y"), ("x", "c")
    return jax.shard_map(
        per_device,
        mesh=fine,
        in_specs=(
            P(every, None),
            P(every, None, None),
            P(every, None),
            P(every, None),
            P(expert, None, None),
        ),
        out_specs=(
            P(every, None),
            P(expert, replica, None),
            P(expert, replica, None),
        ),
        check_vma=False,
    )
```

```python
import jax
import jax.numpy as jnp
from jax import lax
from jax.experimental import pallas as pl
from jax.experimental.pallas import tpu as pltpu
from jax.sharding import PartitionSpec as P

MESH = pl.DeviceIdType.MESH
BF, F32 = jnp.bfloat16, jnp.float32
BLOCK = 128
NZ, NY, NR = 16, 4, 8
EXPERTS = NZ * NY
SLOTS = 18
TOK, WIDTH, HID, TOP = 128, 2048, 704, 6
PADH = 768
ROUTED = TOK * TOP
COLUMN = NZ * SLOTS
SHARE = HID // NR
DC = 256
ND = WIDTH // DC
HALF = NZ // 2
GROUP = HALF * SLOTS
PLANE = NY * SLOTS


def iota(shape, dim):
    return lax.broadcasted_iota(jnp.int32, shape, dim).astype(F32)


def one_where(condition):
    return jnp.where(condition, 1.0, 0.0).astype(BF)


def kernel(
    cot, hid6, routes, nums, w,
    gate_o, scale_o, grad_o,
    G, PK, HZ, YH, HY, hidL, hT, WS, SEL, YS, R, XS, XR, gacc, RK, GS, GM, GO, GR, G2,
    cot_sem, hid_sem, w_sem, own_sem, ylocal, xlocal,
    ring_send, ring_recv, hz_sem, hy_sem, ys_send, ys_recv, xs_send, xs_recv, gy_sem, gz_sem,
):
    expert = lax.axis_index("expert")
    rep = lax.axis_index("replica")
    z = lax.div(expert, NY)
    y = lax.rem(expert, NY)

    def zat(d):
        return lax.rem(z + d, NZ)

    def zpeer(d):
        return (zat(d) * NY + y, rep)

    def ypeer(d):
        return (z * NY + lax.rem(y + d, NY), rep)

    def xpeer(d):
        return (expert, lax.rem(rep + d, NR))

    def remote(src, dst, send, recv, peer):
        return pltpu.make_async_remote_copy(
            src_ref=src, dst_ref=dst, send_sem=send, recv_sem=recv,
            device_id=peer, device_id_type=MESH,
        )

    cot_loads = [
        pltpu.make_async_copy(cot.at[:, pl.ds(j * DC, DC)], G.at[j, z], cot_sem.at[j])
        for j in range(ND)
    ]
    hid_loads = [
        pltpu.make_async_copy(
            hid6.at[k], hidL.at[pl.ds(0, HID), pl.ds(k * TOK, TOK)], hid_sem.at[k]
        )
        for k in range(TOP)
    ]
    w_loads = [
        pltpu.make_async_copy(
            w.at[:, pl.ds(j * DC, DC)], WS.at[j, pl.ds(0, HID), :], w_sem.at[j]
        )
        for j in range(ND)
    ]
    for copy in cot_loads + hid_loads + w_loads:
        copy.start()

    barrier = pltpu.get_barrier_semaphore()
    peers = (
        [zpeer(d) for d in range(1, NZ)]
        + [ypeer(d) for d in range(1, NY)]
        + [xpeer(d) for d in range(1, NR)]
    )
    for peer in peers:
        pl.semaphore_signal(barrier, inc=1, device_id=peer, device_id_type=MESH)
    pl.semaphore_wait(barrier, len(peers))

    steps = (HALF - 1, HALF)

    def ring_copy(way, j, s):
        slot = zat(NZ - s) if way == 0 else zat(s)
        peer = zpeer(1) if way == 0 else zpeer(NZ - 1)
        here = G.at[j, slot]
        return remote(here, here, ring_send.at[way, j], ring_recv.at[way, j, s], peer)

    def ring_arrival(way, j, s):
        slot = zat(NZ - 1 - s) if way == 0 else zat(1 + s)
        peer = zpeer(1) if way == 0 else zpeer(NZ - 1)
        here = G.at[j, slot]
        remote(here, here, ring_send.at[way, j], ring_recv.at[way, j, s], peer).wait_recv()

    for copy in cot_loads:
        copy.wait()
    for j in range(2):
        for way in range(2):
            ring_copy(way, j, 0).start()

    which = iota((EXPERTS, TOK), 0)
    names = [routes[k : k + 1, :].astype(F32) for k in range(TOP)]
    member = jnp.zeros((EXPERTS, TOK), F32)
    for k in range(TOP):
        member = member + jnp.where(which == names[k], 1.0, 0.0)
    earlier = one_where(iota((TOK, TOK), 0) < iota((TOK, TOK), 1))
    before = jnp.dot(member.astype(BF), earlier, preferred_element_type=F32)
    RK[...] = jnp.where(member > 0.5, before, -1.0)
    slot_row = jnp.concatenate(
        [
            names[k] * float(SLOTS)
            + jnp.sum(jnp.where(which == names[k], before, 0.0), axis=0, keepdims=True)
            for k in range(TOP)
        ],
        axis=1,
    )
    n_row = jnp.concatenate([nums[k : k + 1, :].astype(F32) for k in range(TOP)], axis=1)
    n_high = jnp.floor(n_row * (1.0 / 32.0))
    n_low = n_row - 32.0 * n_high
    t_row = jnp.concatenate([iota((1, TOK), 1) + 1.0] * TOP, axis=1)
    extra_row = iota((PADH - HID, ROUTED), 0)
    extra = jnp.where(
        extra_row == 0.0,
        n_high,
        jnp.where(extra_row == 1.0, n_low, jnp.where(extra_row == 2.0, t_row, 0.0)),
    )
    hidL[HID:PADH, :] = extra.astype(BF)
    WS[:, HID:PADH, :] = jnp.zeros((ND, PADH - HID, DC), BF)
    GO[...] = jnp.zeros_like(GO)
    gacc[...] = jnp.zeros_like(gacc)
    for copy in hid_loads:
        copy.wait()

    def pack(i, carry):
        rows = iota((NY * PLANE, 1), 0) + (i * (NY * PLANE)).astype(F32)
        chosen = one_where(rows == slot_row)
        out = lax.dot_general(
            chosen, hidL[...], (((1,), (1,)), ((), ())), preferred_element_type=F32
        )
        PK[pl.ds(i * NY, NY)] = out.reshape(NY, PLANE, PADH).astype(BF)
        return carry

    lax.fori_loop(0, NZ // NY, pack, 0)
    for d in (8, 7, 9, 6, 10, 5, 11, 4, 12, 3, 13, 2, 14, 1, 15):
        remote(PK.at[zat(d)], HZ.at[z], hz_sem.at[0], hz_sem.at[1], zpeer(d)).start()
    own_hz = pltpu.make_async_copy(PK.at[z], HZ.at[z], own_sem.at[0])
    own_hz.start()
    for copy in w_loads:
        copy.wait()

    def own_hy():
        return pltpu.make_async_copy(
            YH.at[y], HY.at[pl.ds(pl.multiple_of(y * COLUMN, COLUMN), COLUMN)], own_sem.at[1]
        )

    def hidden_mid():
        remote(
            HZ.at[pl.ds(0, NZ - 1)], HZ.at[pl.ds(0, NZ - 1)], hz_sem.at[0], hz_sem.at[1], zpeer(1)
        ).wait_recv()
        own_hz.wait()
        out_row = iota((NY * GROUP, 1), 0)
        out_y = jnp.floor((out_row + 0.5) * (1.0 / GROUP))
        rest = out_row - out_y * GROUP
        out_z = jnp.floor((rest + 0.5) * (1.0 / SLOTS))
        out_r = rest - out_z * SLOTS
        source = out_z * PLANE + out_y * SLOTS + out_r
        permute = one_where(iota((NY * GROUP, NY * GROUP), 1) == source)
        for g in range(2):
            block = HZ[g * HALF : (g + 1) * HALF].astype(F32)
            block = block.reshape(HALF * PLANE, PADH).astype(BF)
            out = jnp.dot(permute, block, preferred_element_type=F32)
            token = out[:, HID + 2 : HID + 3]
            target = jnp.where(token > 0.5, token + out_z * TOK - 1.0, -1.0)
            SEL[g] = one_where(iota((NY * GROUP, HALF * TOK), 1) == target)
            rows = out.astype(BF)
            for yy in range(NY):
                YH[yy, g * GROUP : (g + 1) * GROUP, :] = rows[yy * GROUP : (yy + 1) * GROUP]
        mine = HY.at[pl.ds(pl.multiple_of(y * COLUMN, COLUMN), COLUMN)]
        for d in range(1, NY):
            remote(YH.at[lax.rem(y + d, NY)], mine, hy_sem.at[0], hy_sem.at[1], ypeer(d)).start()
        own_hy().start()

    def hidden_end():
        three = HY.at[pl.ds(0, (NY - 1) * COLUMN)]
        remote(three, three, hy_sem.at[0], hy_sem.at[1], ypeer(1)).wait_recv()
        own_hy().wait()

        def turn(i, carry):
            start = pl.multiple_of(i * TOK, TOK)
            rows = HY[pl.ds(start, TOK), :].astype(F32)
            weight = (rows[:, HID : HID + 1] * 32.0 + rows[:, HID + 1 : HID + 2]) * (1.0 / 1024.0)
            hT[:, pl.ds(start, TOK)] = jnp.transpose(rows * weight).astype(BF)
            return carry

        lax.fori_loop(0, NY * COLUMN // TOK, turn, 0)

    def own_y(c):
        return pltpu.make_async_copy(YS.at[c, y], R.at[c, y], ylocal.at[c])

    def own_x(c):
        return pltpu.make_async_copy(XS.at[c, rep], XR.at[c, rep], xlocal.at[c])

    def select(c):
        for way in range(2):
            ring_arrival(way, c, steps[way] - 1)
        for g in range(2):
            block = G[c, g * HALF : (g + 1) * HALF].reshape(HALF * TOK, DC)
            out = jnp.dot(SEL[g], block, preferred_element_type=F32).astype(BF)
            for yy in range(NY):
                YS[c, yy, g * GROUP : (g + 1) * GROUP, :] = out[yy * GROUP : (yy + 1) * GROUP]
        for d in range(1, NY):
            remote(
                YS.at[c, lax.rem(y + d, NY)], R.at[c, y], ys_send.at[c], ys_recv.at[c], ypeer(d)
            ).start()
        own_y(c).start()

    def products(c):
        three = R.at[c, pl.ds(0, NY - 1)]
        remote(three, three, ys_send.at[c], ys_recv.at[c], ypeer(1)).wait_recv()
        own_y(c).wait()

        def part(i, carry):
            start = pl.multiple_of(i * (HID // 2), HID // 2)
            value = jnp.dot(
                hT[pl.ds(start, HID // 2), :],
                R[c].reshape(NY * COLUMN, DC),
                preferred_element_type=F32,
            )
            XS[c, pl.ds(i * (NR // 2), NR // 2)] = value.reshape(NR // 2, SHARE, DC).astype(BF)
            return carry

        lax.fori_loop(0, 2, part, 0)
        for d in range(1, NR):
            remote(
                XS.at[c, lax.rem(rep + d, NR)], XR.at[c, rep], xs_send.at[c], xs_recv.at[c], xpeer(d)
            ).start()
        own_x(c).start()

        def gates(b, carry):
            rows = HY[pl.ds(pl.multiple_of(b * COLUMN, COLUMN), COLUMN), :]
            value = jnp.dot(rows, WS[c], preferred_element_type=F32) * R[c, b].astype(F32)
            total = value[:, :BLOCK]
            for p in range(1, DC // BLOCK):
                total = total + value[:, p * BLOCK : (p + 1) * BLOCK]
            gacc[b] = gacc[b] + total
            return carry

        lax.fori_loop(0, NY, gates, 0)

    def finish(c):
        seven = XR.at[c, pl.ds(0, NR - 1)]
        remote(seven, seven, xs_send.at[c], xs_recv.at[c], xpeer(1)).wait_recv()
        own_x(c).wait()
        first = XR[c, 0].astype(F32)
        total, largest = first, jnp.abs(first)
        for q in range(1, NR):
            value = XR[c, q].astype(F32)
            total = total + value
            largest = jnp.maximum(largest, jnp.abs(value))
        lane = iota((SHARE, BLOCK), 1)
        for p in range(DC // BLOCK):
            cols = slice(p * BLOCK, (p + 1) * BLOCK)
            scale = jnp.max(largest[:, cols], axis=1, keepdims=True) + 1e-6
            start = pl.multiple_of(c * DC + p * BLOCK, BLOCK)
            grad_o[:, pl.ds(start, BLOCK)] = total[:, cols] / scale
            number = (c * (DC // BLOCK) + p).astype(F32)
            scale_o[...] = jnp.where(lane == number, scale, scale_o[...])

    scale_o[...] = jnp.zeros_like(scale_o)

    def own_gy():
        return pltpu.make_async_copy(GS.at[y], GM.at[y], own_sem.at[2])

    def own_gz():
        return pltpu.make_async_copy(GO.at[z], GR.at[z], own_sem.at[3])

    def gate_start():
        row = iota((COLUMN, BLOCK), 0)
        spread = row - SLOTS * jnp.floor((row + 0.5) * (1.0 / SLOTS)) == iota((COLUMN, BLOCK), 1)
        lane = iota((NZ, COLUMN), 1)
        gather = one_where(jnp.floor((lane + 0.5) * (1.0 / SLOTS)) == iota((NZ, COLUMN), 0))
        for yy in range(NY):
            column = jnp.sum(gacc[yy], axis=1, keepdims=True)
            value = jnp.where(spread, column, 0.0)
            total = jnp.zeros((NZ, BLOCK), F32)
            for _ in range(3):
                digit = value.astype(BF)
                total = total + jnp.dot(gather, digit, preferred_element_type=F32)
                value = value - digit.astype(F32)
            GS[yy] = total
        for d in range(1, NY):
            remote(GS.at[lax.rem(y + d, NY)], GM.at[y], gy_sem.at[0], gy_sem.at[1], ypeer(d)).start()
        own_gy().start()

    def gate_mid():
        three = GM.at[pl.ds(0, NY - 1)]
        remote(three, three, gy_sem.at[0], gy_sem.at[1], ypeer(1)).wait_recv()
        own_gy().wait()
        for yy in range(NY):
            for zz in range(NZ):
                GO[zz, yy : yy + 1, :] = GM[yy, zz : zz + 1, :]
        for d in range(1, NZ):
            remote(GO.at[zat(d)], GR.at[z], gz_sem.at[0], gz_sem.at[1], zpeer(d)).start()
        own_gz().start()

    def gate_end():
        most = GR.at[pl.ds(0, NZ - 1)]
        remote(most, most, gz_sem.at[0], gz_sem.at[1], zpeer(1)).wait_recv()
        own_gz().wait()
        for zz in range(NZ):
            G2[zz * NY : (zz + 1) * NY, :] = GR[zz, 0:NY, :]
        table = G2[...]
        ranks = RK[...]
        value = jnp.zeros((EXPERTS, TOK), F32)
        for s in range(SLOTS):
            value = value + jnp.where(ranks == float(s), table[:, s : s + 1], 0.0)
        for k in range(TOP):
            named = routes[k : k + 1, :].astype(F32)
            gate_o[k : k + 1, :] = jnp.sum(
                jnp.where(iota((EXPERTS, TOK), 0) == named, value, 0.0), axis=0, keepdims=True
            )

    def ring_half(m, h):
        for a in (3, 2, 1, 0):
            s = 2 * a + h
            if s == 0:

                @pl.when(m + 2 < ND)
                def _():
                    for way in range(2):
                        ring_copy(way, m + 2, 0).start()

            else:

                @pl.when(jnp.logical_and(m >= a, m - a < ND))
                def _(s=s, a=a):
                    for way in range(2):
                        if s < steps[way]:
                            ring_arrival(way, m - a, s - 1)
                            ring_copy(way, m - a, s).start()

    def body(m, carry):
        ring_half(m, 0)

        @pl.when(jnp.logical_and(m >= 4, m < ND + 4))
        def _():
            select(m - 4)

        @pl.when(m == 4)
        def _():
            hidden_end()

        ring_half(m, 1)

        @pl.when(jnp.logical_and(m >= 5, m < ND + 5))
        def _():
            products(m - 5)

        @pl.when(m == 3)
        def _():
            hidden_mid()

        @pl.when(m == ND + 4)
        def _():
            gate_start()

        @pl.when(m == ND + 5)
        def _():
            gate_mid()

        @pl.when(m >= 6)
        def _():
            finish(m - 6)

        return carry

    lax.fori_loop(0, ND + 6, body, 0)
    gate_end()

    def drain(c, carry):
        for way in range(2):
            sent = G.at[c, pl.ds(0, steps[way])]
            remote(sent, sent, ring_send.at[way, c], ring_recv.at[way, c, 0], zpeer(1)).wait_send()
        three = YS.at[c, pl.ds(0, NY - 1)]
        remote(three, three, ys_send.at[c], ys_recv.at[c], ypeer(1)).wait_send()
        seven = XS.at[c, pl.ds(0, NR - 1)]
        remote(seven, seven, xs_send.at[c], xs_recv.at[c], xpeer(1)).wait_send()
        return carry

    lax.fori_loop(0, ND, drain, 0)
    most = PK.at[pl.ds(0, NZ - 1)]
    remote(most, most, hz_sem.at[0], hz_sem.at[1], zpeer(1)).wait_send()
    three = YH.at[pl.ds(0, NY - 1)]
    remote(three, three, hy_sem.at[0], hy_sem.at[1], ypeer(1)).wait_send()
    three = GS.at[pl.ds(0, NY - 1)]
    remote(three, three, gy_sem.at[0], gy_sem.at[1], ypeer(1)).wait_send()
    most = GO.at[pl.ds(0, NZ - 1)]
    remote(most, most, gz_sem.at[0], gz_sem.at[1], zpeer(1)).wait_send()


def per_device(cotangent, hidden, routes, numerators, w_down):
    whole = pl.BlockSpec(memory_space=pl.ANY)
    vmem = pl.BlockSpec(memory_space=pltpu.VMEM)
    dma = pltpu.SemaphoreType.DMA
    gate, scales, grad = pl.pallas_call(
        kernel,
        out_shape=(
            jax.ShapeDtypeStruct((TOP, TOK), F32),
            jax.ShapeDtypeStruct((SHARE, BLOCK), F32),
            jax.ShapeDtypeStruct((SHARE, WIDTH), F32),
        ),
        in_specs=[whole, whole, vmem, vmem, whole],
        out_specs=(vmem, vmem, vmem),
        scratch_shapes=[
            pltpu.VMEM((ND, NZ, TOK, DC), BF),
            pltpu.VMEM((NZ, PLANE, PADH), BF),
            pltpu.VMEM((NZ, PLANE, PADH), BF),
            pltpu.VMEM((NY, COLUMN, PADH), BF),
            pltpu.VMEM((NY * COLUMN, PADH), BF),
            pltpu.VMEM((PADH, ROUTED), BF),
            pltpu.VMEM((PADH, NY * COLUMN), BF),
            pltpu.VMEM((ND, PADH, DC), BF),
            pltpu.VMEM((2, NY * GROUP, HALF * TOK), BF),
            pltpu.VMEM((ND, NY, COLUMN, DC), BF),
            pltpu.VMEM((ND, NY, COLUMN, DC), BF),
            pltpu.VMEM((ND, NR, SHARE, DC), BF),
            pltpu.VMEM((ND, NR, SHARE, DC), BF),
            pltpu.VMEM((NY, COLUMN, BLOCK), F32),
            pltpu.VMEM((EXPERTS, TOK), F32),
            pltpu.VMEM((NY, NZ, BLOCK), F32),
            pltpu.VMEM((NY, NZ, BLOCK), F32),
            pltpu.VMEM((NZ, 8, BLOCK), F32),
            pltpu.VMEM((NZ, 8, BLOCK), F32),
            pltpu.VMEM((EXPERTS, BLOCK), F32),
            dma((ND,)),
            dma((TOP,)),
            dma((ND,)),
            dma((4,)),
            dma((ND,)),
            dma((ND,)),
            dma((2, ND)),
            dma((2, ND, HALF)),
            dma((2,)),
            dma((2,)),
            dma((ND,)),
            dma((ND,)),
            dma((ND,)),
            dma((ND,)),
            dma((2,)),
            dma((2,)),
        ],
        compiler_params=pltpu.CompilerParams(
            collective_id=0, has_side_effects=True, vmem_limit_bytes=60 * 1024 * 1024
        ),
    )(
        cotangent,
        hidden.transpose(1, 2, 0),
        routes.T,
        numerators.T,
        w_down[0],
    )
    return gate.T, scales[None, :, : WIDTH // BLOCK], grad[None]


def solution(mesh):
    return jax.shard_map(
        per_device,
        mesh=mesh,
        in_specs=(
            P(("expert", "replica"), None),
            P(("expert", "replica"), None, None),
            P(("expert", "replica"), None),
            P(("expert", "replica"), None),
            P("expert", None, None),
        ),
        out_specs=(
            P(("expert", "replica"), None),
            P("expert", "replica", None),
            P("expert", "replica", None),
        ),
        check_vma=False,
    )
```

```python
import jax
import jax.numpy as jnp
from jax import lax
from jax.experimental import pallas as pl
from jax.experimental.pallas import tpu as pltpu
from jax.sharding import PartitionSpec as P

MESH = pl.DeviceIdType.MESH
BF, F32 = jnp.bfloat16, jnp.float32
BLOCK = 128
NZ, NY, NR = 16, 4, 8
EXPERTS = NZ * NY
SLOTS = 18
TOK, WIDTH, HID, TOP = 128, 2048, 704, 6
PADH = 768
ROUTED = TOK * TOP
COLUMN = NZ * SLOTS
SHARE = HID // NR
DC = 256
ND = WIDTH // DC
HALF = NZ // 2
GROUP = HALF * SLOTS
PLANE = NY * SLOTS
STAGGER = 2
FULL = -(-HALF // STAGGER)
TURN = 1


def iota(shape, dim):
    return lax.broadcasted_iota(jnp.int32, shape, dim).astype(F32)


def one_where(condition):
    return jnp.where(condition, 1.0, 0.0).astype(BF)


def kernel(
    cot, hid6, routes, nums, w,
    gate_o, scale_o, grad_o,
    G, PK, HZ, YH, HY, hidL, hT, WS, SEL, YS, R, XS, XR, gacc, RK, GS, GM, GO, GR, G2, VS, scales,
    cot_sem, hid_sem, w_sem, own_sem, ylocal, xlocal,
    ring_send, ring_recv, hz_sem, hy_sem, ys_send, ys_recv, xs_send, xs_recv, gy_sem, gz_sem,
):
    expert = lax.axis_index("expert")
    rep = lax.axis_index("replica")
    z = lax.div(expert, NY)
    y = lax.rem(expert, NY)

    def zat(d):
        return lax.rem(z + d, NZ)

    def zpeer(d):
        return (zat(d) * NY + y, rep)

    def ypeer(d):
        return (z * NY + lax.rem(y + d, NY), rep)

    def xpeer(d):
        return (expert, lax.rem(rep + d, NR))

    def remote(src, dst, send, recv, peer):
        return pltpu.make_async_remote_copy(
            src_ref=src, dst_ref=dst, send_sem=send, recv_sem=recv,
            device_id=peer, device_id_type=MESH,
        )

    cot_loads = [
        pltpu.make_async_copy(cot.at[:, pl.ds(j * DC, DC)], G.at[j, z], cot_sem.at[j])
        for j in range(ND)
    ]
    hid_loads = [
        pltpu.make_async_copy(
            hid6.at[k], hidL.at[pl.ds(0, HID), pl.ds(k * TOK, TOK)], hid_sem.at[k]
        )
        for k in range(TOP)
    ]
    w_loads = [
        pltpu.make_async_copy(
            w.at[:, pl.ds(j * DC, DC)], WS.at[j, pl.ds(0, HID), :], w_sem.at[j]
        )
        for j in range(ND)
    ]
    for copy in cot_loads + hid_loads + w_loads:
        copy.start()

    barrier = pltpu.get_barrier_semaphore()
    peers = (
        [zpeer(d) for d in range(1, NZ)]
        + [ypeer(d) for d in range(1, NY)]
        + [xpeer(d) for d in range(1, NR)]
    )
    for peer in peers:
        pl.semaphore_signal(barrier, inc=1, device_id=peer, device_id_type=MESH)
    pl.semaphore_wait(barrier, len(peers))

    def ring_copy(way, j, s):
        slot = zat(NZ - s) if way == 0 else zat(s)
        peer = zpeer(1) if way == 0 else zpeer(NZ - 1)
        here = G.at[j, slot]
        return remote(here, here, ring_send.at[way, j], ring_recv.at[way, j, s], peer)

    def ring_arrival(way, j, s):
        slot = zat(NZ - 1 - s) if way == 0 else zat(1 + s)
        peer = zpeer(1) if way == 0 else zpeer(NZ - 1)
        here = G.at[j, slot]
        remote(here, here, ring_send.at[way, j], ring_recv.at[way, j, s], peer).wait_recv()

    for j in range(ND):
        cot_loads[j].wait()
        for way in range(2):
            ring_copy(way, j, 0).start()

    which = iota((EXPERTS, TOK), 0)
    names = [routes[k : k + 1, :].astype(F32) for k in range(TOP)]
    member = jnp.zeros((EXPERTS, TOK), F32)
    for k in range(TOP):
        member = member + jnp.where(which == names[k], 1.0, 0.0)
    earlier = one_where(iota((TOK, TOK), 0) < iota((TOK, TOK), 1))
    before = jnp.dot(member.astype(BF), earlier, preferred_element_type=F32)
    RK[...] = jnp.where(member > 0.5, before, -1.0)
    slot_row = jnp.concatenate(
        [
            names[k] * float(SLOTS)
            + jnp.sum(jnp.where(which == names[k], before, 0.0), axis=0, keepdims=True)
            for k in range(TOP)
        ],
        axis=1,
    )
    n_row = jnp.concatenate([nums[k : k + 1, :].astype(F32) for k in range(TOP)], axis=1)
    n_high = jnp.floor(n_row * (1.0 / 32.0))
    n_low = n_row - 32.0 * n_high
    t_row = jnp.concatenate([iota((1, TOK), 1) + 1.0] * TOP, axis=1)
    extra_row = iota((PADH - HID, ROUTED), 0)
    extra = jnp.where(
        extra_row == 0.0,
        n_high,
        jnp.where(extra_row == 1.0, n_low, jnp.where(extra_row == 2.0, t_row, 0.0)),
    )
    hidL[HID:PADH, :] = extra.astype(BF)
    WS[:, HID:PADH, :] = jnp.zeros((ND, PADH - HID, DC), BF)
    GO[...] = jnp.zeros_like(GO)
    gacc[...] = jnp.zeros_like(gacc)
    for copy in hid_loads:
        copy.wait()

    def pack(i, carry):
        rows = iota((NY * PLANE, 1), 0) + (i * (NY * PLANE)).astype(F32)
        chosen = one_where(rows == slot_row)
        out = lax.dot_general(
            chosen, hidL[...], (((1,), (1,)), ((), ())), preferred_element_type=F32
        )
        PK[pl.ds(i * NY, NY)] = out.reshape(NY, PLANE, PADH).astype(BF)
        return carry

    lax.fori_loop(0, NZ // NY, pack, 0)
    for d in (8, 7, 9, 6, 10, 5, 11, 4, 12, 3, 13, 2, 14, 1, 15):
        remote(PK.at[zat(d)], HZ.at[z], hz_sem.at[0], hz_sem.at[1], zpeer(d)).start()
    own_hz = pltpu.make_async_copy(PK.at[z], HZ.at[z], own_sem.at[0])
    own_hz.start()
    for copy in w_loads:
        copy.wait()

    def own_hy():
        return pltpu.make_async_copy(
            YH.at[y], HY.at[pl.ds(pl.multiple_of(y * COLUMN, COLUMN), COLUMN)], own_sem.at[1]
        )

    def hidden_mid():
        remote(
            HZ.at[pl.ds(0, NZ - 1)], HZ.at[pl.ds(0, NZ - 1)], hz_sem.at[0], hz_sem.at[1], zpeer(1)
        ).wait_recv()
        own_hz.wait()
        out_row = iota((NY * GROUP, 1), 0)
        out_y = jnp.floor((out_row + 0.5) * (1.0 / GROUP))
        rest = out_row - out_y * GROUP
        out_z = jnp.floor((rest + 0.5) * (1.0 / SLOTS))
        out_r = rest - out_z * SLOTS
        source = out_z * PLANE + out_y * SLOTS + out_r
        permute = one_where(iota((NY * GROUP, NY * GROUP), 1) == source)
        for g in range(2):
            block = HZ[g * HALF : (g + 1) * HALF].astype(F32)
            block = block.reshape(HALF * PLANE, PADH).astype(BF)
            out = jnp.dot(permute, block, preferred_element_type=F32)
            token = out[:, HID + 2 : HID + 3]
            target = jnp.where(token > 0.5, token + out_z * TOK - 1.0, -1.0)
            SEL[g] = one_where(iota((NY * GROUP, HALF * TOK), 1) == target)
            rows = out.astype(BF)
            for yy in range(NY):
                YH[yy, g * GROUP : (g + 1) * GROUP, :] = rows[yy * GROUP : (yy + 1) * GROUP]
        mine = HY.at[pl.ds(pl.multiple_of(y * COLUMN, COLUMN), COLUMN)]
        for d in range(1, NY):
            remote(YH.at[lax.rem(y + d, NY)], mine, hy_sem.at[0], hy_sem.at[1], ypeer(d)).start()
        own_hy().start()

    def hidden_end():
        three = HY.at[pl.ds(0, (NY - 1) * COLUMN)]
        remote(three, three, hy_sem.at[0], hy_sem.at[1], ypeer(1)).wait_recv()
        own_hy().wait()

        def turn(i, carry):
            start = pl.multiple_of(i * TOK, TOK)
            rows = HY[pl.ds(start, TOK), :].astype(F32)
            weight = (rows[:, HID : HID + 1] * 32.0 + rows[:, HID + 1 : HID + 2]) * (1.0 / 1024.0)
            hT[:, pl.ds(start, TOK)] = jnp.transpose(rows * weight).astype(BF)
            return carry

        lax.fori_loop(0, NY * COLUMN // TOK, turn, 0)

    def drain_ring(c, carry):
        for way in range(2):
            sent = G.at[c, pl.ds(0, HALF - 1)]
            remote(sent, sent, ring_send.at[way, c], ring_recv.at[way, c, 0], zpeer(1)).wait_send()

            @pl.when(lax.rem(c + way, 2) == 1)
            def _(way=way):
                more = G.at[c, 0]
                remote(more, more, ring_send.at[way, c], ring_recv.at[way, c, 0], zpeer(1)).wait_send()

        return carry

    def drain_rows(c, carry):
        three = YS.at[c, pl.ds(0, NY - 1)]
        remote(three, three, ys_send.at[c], ys_recv.at[c], ypeer(1)).wait_send()
        return carry

    def drain_parts(c, carry):
        seven = XS.at[c, pl.ds(0, NR - 1)]
        remote(seven, seven, xs_send.at[c], xs_recv.at[c], xpeer(1)).wait_send()
        return carry

    def own_y(c):
        return pltpu.make_async_copy(YS.at[c, y], R.at[c, y], ylocal.at[c])

    def own_x(c):
        return pltpu.make_async_copy(XS.at[c, rep], XR.at[c, rep], xlocal.at[c])

    def select(c):
        for way in range(2):

            @pl.when(lax.rem(c + way, 2) == 1)
            def _(way=way):
                ring_arrival(way, c, HALF - 1)
                ring_arrival(1 - way, c, HALF - 2)

        for g in range(2):
            block = G[c, g * HALF : (g + 1) * HALF].reshape(HALF * TOK, DC)
            out = jnp.dot(SEL[g], block, preferred_element_type=F32).astype(BF)
            for yy in range(NY):
                YS[c, yy, g * GROUP : (g + 1) * GROUP, :] = out[yy * GROUP : (yy + 1) * GROUP]
        for d in range(1, NY):
            remote(
                YS.at[c, lax.rem(y + d, NY)], R.at[c, y], ys_send.at[c], ys_recv.at[c], ypeer(d)
            ).start()
        own_y(c).start()

    def products(c):
        def ahead(b, carry):
            rows = HY[pl.ds(pl.multiple_of(b * COLUMN, COLUMN), COLUMN), :]
            VS[b] = jnp.dot(rows, WS[c], preferred_element_type=F32)
            return carry

        lax.fori_loop(0, NY, ahead, 0)

        @pl.when(c == ND - 1)
        def _():
            lax.fori_loop(0, ND, drain_ring, 0)
            lax.fori_loop(0, ND - 1, drain_rows, 0)
            most = PK.at[pl.ds(0, NZ - 1)]
            remote(most, most, hz_sem.at[0], hz_sem.at[1], zpeer(1)).wait_send()
            half = YH.at[pl.ds(0, NY - 1)]
            remote(half, half, hy_sem.at[0], hy_sem.at[1], ypeer(1)).wait_send()

        three = R.at[c, pl.ds(0, NY - 1)]
        remote(three, three, ys_send.at[c], ys_recv.at[c], ypeer(1)).wait_recv()
        own_y(c).wait()

        def gates(b, carry):
            value = VS[b] * R[c, b].astype(F32)
            total = value[:, :BLOCK]
            for p in range(1, DC // BLOCK):
                total = total + value[:, p * BLOCK : (p + 1) * BLOCK]
            gacc[b] = gacc[b] + total
            return carry

        lax.fori_loop(0, NY, gates, 0)

        @pl.when(c == ND - 1)
        def _():
            gate_start()

        def part(i, carry):
            start = pl.multiple_of(i * (HID // 2), HID // 2)
            value = jnp.dot(
                hT[pl.ds(start, HID // 2), :],
                R[c].reshape(NY * COLUMN, DC),
                preferred_element_type=F32,
            )
            XS[c, pl.ds(i * (NR // 2), NR // 2)] = value.reshape(NR // 2, SHARE, DC).astype(BF)
            return carry

        lax.fori_loop(0, 2, part, 0)
        for d in range(1, NR):
            remote(
                XS.at[c, lax.rem(rep + d, NR)], XR.at[c, rep], xs_send.at[c], xs_recv.at[c], xpeer(d)
            ).start()
        own_x(c).start()

    def finish(c):
        seven = XR.at[c, pl.ds(0, NR - 1)]
        remote(seven, seven, xs_send.at[c], xs_recv.at[c], xpeer(1)).wait_recv()
        own_x(c).wait()
        first = XR[c, 0].astype(F32)
        total, largest = first, jnp.abs(first)
        for q in range(1, NR):
            value = XR[c, q].astype(F32)
            total = total + value
            largest = jnp.maximum(largest, jnp.abs(value))
        for p in range(DC // BLOCK):
            cols = slice(p * BLOCK, (p + 1) * BLOCK)
            scale = jnp.max(largest[:, cols], axis=1, keepdims=True) + 1e-6
            start = pl.multiple_of(c * DC + p * BLOCK, BLOCK)
            grad_o[:, pl.ds(start, BLOCK)] = total[:, cols] / scale
            number = (c * (DC // BLOCK) + p).astype(F32)
            scales[...] = jnp.where(iota((SHARE, BLOCK), 1) == number, scale, scales[...])

    scales[...] = jnp.zeros_like(scales)

    def own_gy():
        return pltpu.make_async_copy(GS.at[y], GM.at[y], own_sem.at[2])

    def own_gz():
        return pltpu.make_async_copy(GO.at[z], GR.at[z], own_sem.at[3])

    def gate_start():
        row = iota((COLUMN, BLOCK), 0)
        spread = row - SLOTS * jnp.floor((row + 0.5) * (1.0 / SLOTS)) == iota((COLUMN, BLOCK), 1)
        lane = iota((NZ, COLUMN), 1)
        gather = one_where(jnp.floor((lane + 0.5) * (1.0 / SLOTS)) == iota((NZ, COLUMN), 0))
        for yy in range(NY):
            column = jnp.sum(gacc[yy], axis=1, keepdims=True)
            value = jnp.where(spread, column, 0.0)
            total = jnp.zeros((NZ, BLOCK), F32)
            for _ in range(3):
                digit = value.astype(BF)
                total = total + jnp.dot(gather, digit, preferred_element_type=F32)
                value = value - digit.astype(F32)
            GS[yy] = total
        for d in range(1, NY):
            remote(GS.at[lax.rem(y + d, NY)], GM.at[y], gy_sem.at[0], gy_sem.at[1], ypeer(d)).start()
        own_gy().start()

    def gate_mid():
        three = GM.at[pl.ds(0, NY - 1)]
        remote(three, three, gy_sem.at[0], gy_sem.at[1], ypeer(1)).wait_recv()
        own_gy().wait()
        for yy in range(NY):
            for zz in range(NZ):
                GO[zz, yy : yy + 1, :] = GM[yy, zz : zz + 1, :]
        for d in range(1, NZ):
            remote(GO.at[zat(d)], GR.at[z], gz_sem.at[0], gz_sem.at[1], zpeer(d)).start()
        own_gz().start()

    def gate_end():
        most = GR.at[pl.ds(0, NZ - 1)]
        remote(most, most, gz_sem.at[0], gz_sem.at[1], zpeer(1)).wait_recv()
        own_gz().wait()
        for zz in range(NZ):
            G2[zz * NY : (zz + 1) * NY, :] = GR[zz, 0:NY, :]
        table = G2[...]
        ranks = RK[...]
        value = jnp.zeros((EXPERTS, TOK), F32)
        for s in range(SLOTS):
            value = value + jnp.where(ranks == float(s), table[:, s : s + 1], 0.0)
        for k in range(TOP):
            named = routes[k : k + 1, :].astype(F32)
            gate_o[k : k + 1, :] = jnp.sum(
                jnp.where(iota((EXPERTS, TOK), 0) == named, value, 0.0), axis=0, keepdims=True
            )

    last = HALF - 1

    def ring_steps(m, h):
        for s in range(last, 0, -1):
            if s % STAGGER != h:
                continue
            j = m - s // STAGGER
            valid = jnp.logical_and(j >= 0, j < ND)

            if s < last:

                @pl.when(valid)
                def _(s=s, j=j):
                    for way in range(2):
                        ring_arrival(way, j, s - 1)
                        ring_copy(way, j, s).start()

            else:
                for way in range(2):

                    @pl.when(jnp.logical_and(valid, lax.rem(j + way, 2) == 1))
                    def _(s=s, j=j, way=way):
                        ring_arrival(way, j, s - 1)
                        ring_copy(way, j, s).start()

    def body(m, carry):
        ring_steps(m, 0)

        @pl.when(jnp.logical_and(m >= FULL, m < ND + FULL))
        def _():
            select(m - FULL)

        @pl.when(m == FULL)
        def _():
            hidden_end()

        for h in range(1, STAGGER):
            ring_steps(m, h)

        @pl.when(jnp.logical_and(m >= FULL + 1, m < ND + FULL + 1))
        def _():
            products(m - FULL - 1)

        @pl.when(m == TURN)
        def _():
            hidden_mid()

        @pl.when(m == ND + FULL + 1)
        def _():
            gate_mid()
            lax.fori_loop(0, ND - 1, drain_parts, 0)

        @pl.when(m >= FULL + 2)
        def _():
            finish(m - FULL - 2)

        return carry

    lax.fori_loop(0, ND + FULL + 2, body, 0)
    gate_end()

    scale_o[...] = jnp.transpose(scales[...])[: WIDTH // BLOCK, :]
    lax.fori_loop(ND - 1, ND, drain_rows, 0)
    lax.fori_loop(ND - 1, ND, drain_parts, 0)
    three = GS.at[pl.ds(0, NY - 1)]
    remote(three, three, gy_sem.at[0], gy_sem.at[1], ypeer(1)).wait_send()
    most = GO.at[pl.ds(0, NZ - 1)]
    remote(most, most, gz_sem.at[0], gz_sem.at[1], zpeer(1)).wait_send()


def per_device(cotangent, hidden, routes, numerators, w_down):
    whole = pl.BlockSpec(memory_space=pl.ANY)
    vmem = pl.BlockSpec(memory_space=pltpu.VMEM)
    dma = pltpu.SemaphoreType.DMA
    gate, scales, grad = pl.pallas_call(
        kernel,
        out_shape=(
            jax.ShapeDtypeStruct((TOP, TOK), F32),
            jax.ShapeDtypeStruct((WIDTH // BLOCK, SHARE), F32),
            jax.ShapeDtypeStruct((SHARE, WIDTH), F32),
        ),
        in_specs=[whole, whole, vmem, vmem, whole],
        out_specs=(vmem, vmem, vmem),
        scratch_shapes=[
            pltpu.VMEM((ND, NZ, TOK, DC), BF),
            pltpu.VMEM((NZ, PLANE, PADH), BF),
            pltpu.VMEM((NZ, PLANE, PADH), BF),
            pltpu.VMEM((NY, COLUMN, PADH), BF),
            pltpu.VMEM((NY * COLUMN, PADH), BF),
            pltpu.VMEM((PADH, ROUTED), BF),
            pltpu.VMEM((PADH, NY * COLUMN), BF),
            pltpu.VMEM((ND, PADH, DC), BF),
            pltpu.VMEM((2, NY * GROUP, HALF * TOK), BF),
            pltpu.VMEM((ND, NY, COLUMN, DC), BF),
            pltpu.VMEM((ND, NY, COLUMN, DC), BF),
            pltpu.VMEM((ND, NR, SHARE, DC), BF),
            pltpu.VMEM((ND, NR, SHARE, DC), BF),
            pltpu.VMEM((NY, COLUMN, BLOCK), F32),
            pltpu.VMEM((EXPERTS, TOK), F32),
            pltpu.VMEM((NY, NZ, BLOCK), F32),
            pltpu.VMEM((NY, NZ, BLOCK), F32),
            pltpu.VMEM((NZ, 8, BLOCK), F32),
            pltpu.VMEM((NZ, 8, BLOCK), F32),
            pltpu.VMEM((EXPERTS, BLOCK), F32),
            pltpu.VMEM((NY, COLUMN, DC), F32),
            pltpu.VMEM((SHARE, BLOCK), F32),
            dma((ND,)),
            dma((TOP,)),
            dma((ND,)),
            dma((4,)),
            dma((ND,)),
            dma((ND,)),
            dma((2, ND)),
            dma((2, ND, HALF)),
            dma((2,)),
            dma((2,)),
            dma((ND,)),
            dma((ND,)),
            dma((ND,)),
            dma((ND,)),
            dma((2,)),
            dma((2,)),
        ],
        compiler_params=pltpu.CompilerParams(
            collective_id=0, has_side_effects=True, vmem_limit_bytes=60 * 1024 * 1024
        ),
    )(
        cotangent,
        hidden.transpose(1, 2, 0),
        routes.T,
        numerators.T,
        w_down[0],
    )
    return gate.T, scales.T[None], grad[None]


def solution(mesh):
    return jax.shard_map(
        per_device,
        mesh=mesh,
        in_specs=(
            P(("expert", "replica"), None),
            P(("expert", "replica"), None, None),
            P(("expert", "replica"), None),
            P(("expert", "replica"), None),
            P("expert", None, None),
        ),
        out_specs=(
            P(("expert", "replica"), None),
            P("expert", "replica", None),
            P("expert", "replica", None),
        ),
        check_vma=False,
    )
```

```python
import jax
import jax.numpy as jnp
from jax import lax
from jax.experimental import pallas as pl
from jax.experimental.pallas import tpu as pltpu
from jax.sharding import PartitionSpec as P

MESH = pl.DeviceIdType.MESH
BF, F32 = jnp.bfloat16, jnp.float32
BLOCK = 128
NZ, NY, NR = 16, 4, 8
EXPERTS = NZ * NY
SLOTS = 18
TOK, WIDTH, HID, TOP = 128, 2048, 704, 6
PADH = 768
MAIN = 640
LOW = 40
CODES = 3
ROUTED = TOK * TOP
COLUMN = NZ * SLOTS
SHARE = HID // NR
DC = 256
ND = WIDTH // DC
HALF = NZ // 2
GROUP = HALF * SLOTS
PLANE = NY * SLOTS
STAGGER = 2
FULL = -(-HALF // STAGGER)
TURN = 1


def iota(shape, dim):
    return lax.broadcasted_iota(jnp.int32, shape, dim).astype(F32)


def one_where(condition):
    return jnp.where(condition, 1.0, 0.0).astype(BF)


def kernel(
    cot, hid6, routes_in, nums_in, w,
    gate_o, scale_o, grad_o,
    G, PK, HZ, YH, HY, hidL, hT, WS, SEL, YS, R, XS, XR, gacc, RK, GS, GM, GO, GR, G2, VS, scales, PT, TZ, ENDS, routes, nums,
    cot_sem, hid_sem, w_sem, own_sem, ylocal, xlocal,
    ring_send, ring_recv, hz_sem, hy_sem, ys_send, ys_recv, xs_send, xs_recv, gy_sem, gz_sem, ht_sem,
):
    expert = lax.axis_index("expert")
    rep = lax.axis_index("replica")
    z = lax.div(expert, NY)
    y = lax.rem(expert, NY)

    def zat(d):
        return lax.rem(z + d, NZ)

    def zpeer(d):
        return (zat(d) * NY + y, rep)

    def ypeer(d):
        return (z * NY + lax.rem(y + d, NY), rep)

    def xpeer(d):
        return (expert, lax.rem(rep + d, NR))

    def remote(src, dst, send, recv, peer):
        return pltpu.make_async_remote_copy(
            src_ref=src, dst_ref=dst, send_sem=send, recv_sem=recv,
            device_id=peer, device_id_type=MESH,
        )

    cot_loads = [
        pltpu.make_async_copy(cot.at[:, pl.ds(j * DC, DC)], G.at[j, z], cot_sem.at[j])
        for j in range(ND)
    ]
    hid_loads = [
        pltpu.make_async_copy(
            hid6.at[k], hidL.at[pl.ds(0, HID), pl.ds(k * TOK, TOK)], hid_sem.at[k]
        )
        for k in range(TOP)
    ]
    w_loads = [
        pltpu.make_async_copy(
            w.at[:, pl.ds(j * DC, DC)], WS.at[j, pl.ds(0, HID), :], w_sem.at[j]
        )
        for j in range(ND)
    ]
    small_loads = [
        pltpu.make_async_copy(routes_in, routes, own_sem.at[5]),
        pltpu.make_async_copy(nums_in, nums, own_sem.at[6]),
    ]
    for copy in small_loads + cot_loads + hid_loads + w_loads:
        copy.start()

    barrier = pltpu.get_barrier_semaphore()
    peers = (
        [zpeer(d) for d in range(1, NZ)]
        + [ypeer(d) for d in range(1, NY)]
        + [xpeer(d) for d in range(1, NR)]
    )
    for peer in peers:
        pl.semaphore_signal(barrier, inc=1, device_id=peer, device_id_type=MESH)
    pl.semaphore_wait(barrier, len(peers))

    def ring_copy(way, j, s):
        slot = zat(NZ - s) if way == 0 else zat(s)
        peer = zpeer(1) if way == 0 else zpeer(NZ - 1)
        here = G.at[j, slot]
        return remote(here, here, ring_send.at[way, j], ring_recv.at[way, j, s], peer)

    def ring_arrival(way, j, s):
        slot = zat(NZ - 1 - s) if way == 0 else zat(1 + s)
        peer = zpeer(1) if way == 0 else zpeer(NZ - 1)
        here = G.at[j, slot]
        remote(here, here, ring_send.at[way, j], ring_recv.at[way, j, s], peer).wait_recv()

    for j in range(ND):
        cot_loads[j].wait()
        for way in range(2):
            ring_copy(way, j, 0).start()

    for copy in small_loads:
        copy.wait()
    which = iota((EXPERTS, TOK), 0)
    names = [routes[k : k + 1, :].astype(F32) for k in range(TOP)]
    member = jnp.zeros((EXPERTS, TOK), F32)
    for k in range(TOP):
        member = member + jnp.where(which == names[k], 1.0, 0.0)
    earlier = one_where(iota((TOK, TOK), 0) < iota((TOK, TOK), 1))
    before = jnp.dot(member.astype(BF), earlier, preferred_element_type=F32)
    RK[...] = jnp.where(member > 0.5, before, -1.0)
    slot_row = jnp.concatenate(
        [
            names[k] * float(SLOTS)
            + jnp.sum(jnp.where(which == names[k], before, 0.0), axis=0, keepdims=True)
            for k in range(TOP)
        ],
        axis=1,
    )
    n_row = jnp.concatenate([nums[k : k + 1, :].astype(F32) for k in range(TOP)], axis=1)
    n_high = jnp.floor(n_row * (1.0 / 32.0))
    n_low = n_row - 32.0 * n_high
    t_row = jnp.concatenate([iota((1, TOK), 1) + 1.0] * TOP, axis=1)
    extra_row = iota((PADH - HID, ROUTED), 0)
    extra = jnp.where(
        extra_row == 0.0,
        n_high,
        jnp.where(extra_row == 1.0, n_low, jnp.where(extra_row == 2.0, t_row, 0.0)),
    )
    hidL[HID:PADH, :] = extra.astype(BF)
    WS[:, HID:PADH, :] = jnp.zeros((ND, PADH - HID, DC), BF)
    GO[...] = jnp.zeros_like(GO)
    gacc[...] = jnp.zeros_like(gacc)
    for copy in hid_loads:
        copy.wait()

    def pack(i, carry):
        rows = iota((NY * PLANE, 1), 0) + (i * (NY * PLANE)).astype(F32)
        chosen = one_where(rows == slot_row)
        out = lax.dot_general(
            chosen, hidL[...], (((1,), (1,)), ((), ())), preferred_element_type=F32
        )
        PK[pl.ds(i * NY, NY)] = out[:, :MAIN].reshape(NY, PLANE, MAIN).astype(BF)
        ends = out[:, MAIN:].reshape(NY, PLANE, BLOCK)
        lane = iota((NY, 8, BLOCK), 2)
        codes = jnp.zeros((NY, 8, BLOCK), F32)
        for q in range(PLANE // 8):
            first = BLOCK // 2 + CODES * q
            moved = pltpu.roll(ends[:, 8 * q : 8 * q + 8, :], CODES * q, 2)
            here = jnp.logical_and(lane >= first, lane < first + CODES)
            codes = codes + jnp.where(here, moved, 0.0)
        for q in range(LOW // 8):
            low = ends[:, 8 * q : 8 * q + 8, :]
            if 8 * q + LOW < PLANE:
                start = 8 * q + LOW
                high = pltpu.roll(ends[:, start : start + 8, :], BLOCK // 2, 2)
            else:
                high = codes
            line = jnp.where(lane < BLOCK // 2, low, high)
            PT[pl.ds(i * NY, NY), 8 * q : 8 * q + 8, :] = line.astype(BF)
        return carry

    lax.fori_loop(0, NZ // NY, pack, 0)
    for d in (8, 7, 9, 6, 10, 5, 11, 4, 12, 3, 13, 2, 14, 1, 15):
        remote(PK.at[zat(d)], HZ.at[z], hz_sem.at[0], hz_sem.at[1], zpeer(d)).start()
        remote(PT.at[zat(d)], TZ.at[z], ht_sem.at[0], ht_sem.at[1], zpeer(d)).start()
    own_hz = pltpu.make_async_copy(PK.at[z], HZ.at[z], own_sem.at[0])
    own_hz.start()
    own_tz = pltpu.make_async_copy(PT.at[z], TZ.at[z], own_sem.at[4])
    own_tz.start()
    for copy in w_loads:
        copy.wait()

    def own_hy():
        return pltpu.make_async_copy(
            YH.at[y], HY.at[pl.ds(pl.multiple_of(y * COLUMN, COLUMN), COLUMN)], own_sem.at[1]
        )

    def hidden_mid():
        remote(
            HZ.at[pl.ds(0, NZ - 1)], HZ.at[pl.ds(0, NZ - 1)], hz_sem.at[0], hz_sem.at[1], zpeer(1)
        ).wait_recv()
        own_hz.wait()
        most = TZ.at[pl.ds(0, NZ - 1)]
        remote(most, most, ht_sem.at[0], ht_sem.at[1], zpeer(1)).wait_recv()
        own_tz.wait()
        out_row = iota((NY * GROUP, 1), 0)
        out_y = jnp.floor((out_row + 0.5) * (1.0 / GROUP))
        rest = out_row - out_y * GROUP
        out_z = jnp.floor((rest + 0.5) * (1.0 / SLOTS))
        out_r = rest - out_z * SLOTS
        source = out_z * PLANE + out_y * SLOTS + out_r
        permute = one_where(iota((NY * GROUP, NY * GROUP), 1) == source)
        for g in range(2):
            block = HZ[g * HALF : (g + 1) * HALF].astype(F32)
            lines = TZ[g * HALF : (g + 1) * HALF].astype(F32)
            lane = iota((HALF, 8, BLOCK), 2)
            for q in range(PLANE // 8):
                start = 8 * q if 8 * q < LOW else 8 * q - LOW
                values = lines[:, start : start + 8, :]
                if 8 * q >= LOW:
                    values = pltpu.roll(values, BLOCK // 2, 2)
                codes = pltpu.roll(lines[:, LOW - 8 : LOW, :], (BLOCK - CODES * q) % BLOCK, 2)
                kept = jnp.where(lane < BLOCK // 2 + CODES, codes, 0.0)
                ENDS[:, 8 * q : 8 * q + 8, :] = jnp.where(lane < BLOCK // 2, values, kept)
            main = block.reshape(HALF * PLANE, MAIN).astype(BF)
            ends = ENDS[...].reshape(HALF * PLANE, BLOCK).astype(BF)
            out = jnp.concatenate(
                [
                    jnp.dot(permute, main, preferred_element_type=F32),
                    jnp.dot(permute, ends, preferred_element_type=F32),
                ],
                axis=1,
            )
            token = out[:, HID + 2 : HID + 3]
            target = jnp.where(token > 0.5, token + out_z * TOK - 1.0, -1.0)
            SEL[g] = one_where(iota((NY * GROUP, HALF * TOK), 1) == target)
            rows = out.astype(BF)
            for yy in range(NY):
                YH[yy, g * GROUP : (g + 1) * GROUP, :] = rows[yy * GROUP : (yy + 1) * GROUP]
        mine = HY.at[pl.ds(pl.multiple_of(y * COLUMN, COLUMN), COLUMN)]
        for d in range(1, NY):
            remote(YH.at[lax.rem(y + d, NY)], mine, hy_sem.at[0], hy_sem.at[1], ypeer(d)).start()
        own_hy().start()

    def hidden_end():
        three = HY.at[pl.ds(0, (NY - 1) * COLUMN)]
        remote(three, three, hy_sem.at[0], hy_sem.at[1], ypeer(1)).wait_recv()
        own_hy().wait()

        def turn(i, carry):
            start = pl.multiple_of(i * TOK, TOK)
            rows = HY[pl.ds(start, TOK), :].astype(F32)
            weight = (rows[:, HID : HID + 1] * 32.0 + rows[:, HID + 1 : HID + 2]) * (1.0 / 1024.0)
            hT[:, pl.ds(start, TOK)] = jnp.transpose(rows * weight).astype(BF)
            return carry

        lax.fori_loop(0, NY * COLUMN // TOK, turn, 0)

    def drain_ring(c, carry):
        for way in range(2):
            sent = G.at[c, pl.ds(0, HALF - 1)]
            remote(sent, sent, ring_send.at[way, c], ring_recv.at[way, c, 0], zpeer(1)).wait_send()

            @pl.when(lax.rem(c + way, 2) == 1)
            def _(way=way):
                more = G.at[c, 0]
                remote(more, more, ring_send.at[way, c], ring_recv.at[way, c, 0], zpeer(1)).wait_send()

        return carry

    def drain_rows(c, carry):
        three = YS.at[c, pl.ds(0, NY - 1)]
        remote(three, three, ys_send.at[c], ys_recv.at[c], ypeer(1)).wait_send()
        return carry

    def drain_parts(c, carry):
        seven = XS.at[c, pl.ds(0, NR - 1)]
        remote(seven, seven, xs_send.at[c], xs_recv.at[c], xpeer(1)).wait_send()
        return carry

    def own_y(c):
        return pltpu.make_async_copy(YS.at[c, y], R.at[c, y], ylocal.at[c])

    def own_x(c):
        return pltpu.make_async_copy(XS.at[c, rep], XR.at[c, rep], xlocal.at[c])

    def select(c):
        for way in range(2):

            @pl.when(lax.rem(c + way, 2) == 1)
            def _(way=way):
                ring_arrival(way, c, HALF - 1)
                ring_arrival(1 - way, c, HALF - 2)

        for g in range(2):
            block = G[c, g * HALF : (g + 1) * HALF].reshape(HALF * TOK, DC)
            out = jnp.dot(SEL[g], block, preferred_element_type=F32).astype(BF)
            for yy in range(NY):
                YS[c, yy, g * GROUP : (g + 1) * GROUP, :] = out[yy * GROUP : (yy + 1) * GROUP]
        for d in range(1, NY):
            remote(
                YS.at[c, lax.rem(y + d, NY)], R.at[c, y], ys_send.at[c], ys_recv.at[c], ypeer(d)
            ).start()
        own_y(c).start()

    def products(c):
        def ahead(b, carry):
            rows = HY[pl.ds(pl.multiple_of(b * COLUMN, COLUMN), COLUMN), :]
            VS[b] = jnp.dot(rows, WS[c], preferred_element_type=F32)
            return carry

        lax.fori_loop(0, NY, ahead, 0)

        @pl.when(c == ND - 1)
        def _():
            lax.fori_loop(0, ND, drain_ring, 0)
            lax.fori_loop(0, ND - 1, drain_rows, 0)
            most = PK.at[pl.ds(0, NZ - 1)]
            remote(most, most, hz_sem.at[0], hz_sem.at[1], zpeer(1)).wait_send()
            most = PT.at[pl.ds(0, NZ - 1)]
            remote(most, most, ht_sem.at[0], ht_sem.at[1], zpeer(1)).wait_send()
            half = YH.at[pl.ds(0, NY - 1)]
            remote(half, half, hy_sem.at[0], hy_sem.at[1], ypeer(1)).wait_send()

        three = R.at[c, pl.ds(0, NY - 1)]
        remote(three, three, ys_send.at[c], ys_recv.at[c], ypeer(1)).wait_recv()
        own_y(c).wait()

        def gates(b, carry):
            value = VS[b] * R[c, b].astype(F32)
            total = value[:, :BLOCK]
            for p in range(1, DC // BLOCK):
                total = total + value[:, p * BLOCK : (p + 1) * BLOCK]
            gacc[b] = gacc[b] + total
            return carry

        lax.fori_loop(0, NY, gates, 0)

        @pl.when(c == ND - 1)
        def _():
            gate_start()

        def part(i, carry):
            start = pl.multiple_of(i * (HID // 2), HID // 2)
            value = jnp.dot(
                hT[pl.ds(start, HID // 2), :],
                R[c].reshape(NY * COLUMN, DC),
                preferred_element_type=F32,
            )
            XS[c, pl.ds(i * (NR // 2), NR // 2)] = value.reshape(NR // 2, SHARE, DC).astype(BF)
            return carry

        lax.fori_loop(0, 2, part, 0)
        for d in range(1, NR):
            remote(
                XS.at[c, lax.rem(rep + d, NR)], XR.at[c, rep], xs_send.at[c], xs_recv.at[c], xpeer(d)
            ).start()
        own_x(c).start()

    def finish(c):
        seven = XR.at[c, pl.ds(0, NR - 1)]
        remote(seven, seven, xs_send.at[c], xs_recv.at[c], xpeer(1)).wait_recv()
        own_x(c).wait()
        first = XR[c, 0].astype(F32)
        total, largest = first, jnp.abs(first)
        for q in range(1, NR):
            value = XR[c, q].astype(F32)
            total = total + value
            largest = jnp.maximum(largest, jnp.abs(value))
        for p in range(DC // BLOCK):
            cols = slice(p * BLOCK, (p + 1) * BLOCK)
            scale = jnp.max(largest[:, cols], axis=1, keepdims=True) + 1e-6
            start = pl.multiple_of(c * DC + p * BLOCK, BLOCK)
            grad_o[:, pl.ds(start, BLOCK)] = total[:, cols] / scale
            number = (c * (DC // BLOCK) + p).astype(F32)
            scales[...] = jnp.where(iota((SHARE, BLOCK), 1) == number, scale, scales[...])

    scales[...] = jnp.zeros_like(scales)

    def own_gy():
        return pltpu.make_async_copy(GS.at[y], GM.at[y], own_sem.at[2])

    def own_gz():
        return pltpu.make_async_copy(GO.at[z], GR.at[z], own_sem.at[3])

    def gate_start():
        row = iota((COLUMN, BLOCK), 0)
        spread = row - SLOTS * jnp.floor((row + 0.5) * (1.0 / SLOTS)) == iota((COLUMN, BLOCK), 1)
        lane = iota((NZ, COLUMN), 1)
        gather = one_where(jnp.floor((lane + 0.5) * (1.0 / SLOTS)) == iota((NZ, COLUMN), 0))
        for yy in range(NY):
            column = jnp.sum(gacc[yy], axis=1, keepdims=True)
            value = jnp.where(spread, column, 0.0)
            total = jnp.zeros((NZ, BLOCK), F32)
            for _ in range(3):
                digit = value.astype(BF)
                total = total + jnp.dot(gather, digit, preferred_element_type=F32)
                value = value - digit.astype(F32)
            GS[yy] = total
        for d in range(1, NY):
            remote(GS.at[lax.rem(y + d, NY)], GM.at[y], gy_sem.at[0], gy_sem.at[1], ypeer(d)).start()
        own_gy().start()

    def gate_mid():
        three = GM.at[pl.ds(0, NY - 1)]
        remote(three, three, gy_sem.at[0], gy_sem.at[1], ypeer(1)).wait_recv()
        own_gy().wait()
        for yy in range(NY):
            for zz in range(NZ):
                GO[zz, yy : yy + 1, :] = GM[yy, zz : zz + 1, :]
        for d in range(1, NZ):
            remote(GO.at[zat(d)], GR.at[z], gz_sem.at[0], gz_sem.at[1], zpeer(d)).start()
        own_gz().start()

    def gate_end():
        most = GR.at[pl.ds(0, NZ - 1)]
        remote(most, most, gz_sem.at[0], gz_sem.at[1], zpeer(1)).wait_recv()
        own_gz().wait()
        for zz in range(NZ):
            G2[zz * NY : (zz + 1) * NY, :] = GR[zz, 0:NY, :]
        table = G2[...]
        ranks = RK[...]
        value = jnp.zeros((EXPERTS, TOK), F32)
        for s in range(SLOTS):
            value = value + jnp.where(ranks == float(s), table[:, s : s + 1], 0.0)
        for k in range(TOP):
            named = routes[k : k + 1, :].astype(F32)
            gate_o[k : k + 1, :] = jnp.sum(
                jnp.where(iota((EXPERTS, TOK), 0) == named, value, 0.0), axis=0, keepdims=True
            )

    last = HALF - 1

    def ring_steps(m, h):
        for s in range(last, 0, -1):
            if s % STAGGER != h:
                continue
            j = m - s // STAGGER
            valid = jnp.logical_and(j >= 0, j < ND)

            if s < last:

                @pl.when(valid)
                def _(s=s, j=j):
                    for way in range(2):
                        ring_arrival(way, j, s - 1)
                        ring_copy(way, j, s).start()

            else:
                for way in range(2):

                    @pl.when(jnp.logical_and(valid, lax.rem(j + way, 2) == 1))
                    def _(s=s, j=j, way=way):
                        ring_arrival(way, j, s - 1)
                        ring_copy(way, j, s).start()

    def body(m, carry):
        ring_steps(m, 0)

        @pl.when(jnp.logical_and(m >= FULL, m < ND + FULL))
        def _():
            select(m - FULL)

        @pl.when(m == FULL)
        def _():
            hidden_end()

        for h in range(1, STAGGER):
            ring_steps(m, h)

        @pl.when(jnp.logical_and(m >= FULL + 1, m < ND + FULL + 1))
        def _():
            products(m - FULL - 1)

        @pl.when(m == TURN)
        def _():
            hidden_mid()

        @pl.when(m == ND + FULL + 1)
        def _():
            gate_mid()
            lax.fori_loop(0, ND - 1, drain_parts, 0)

        @pl.when(m >= FULL + 2)
        def _():
            finish(m - FULL - 2)

        return carry

    lax.fori_loop(0, ND + FULL + 2, body, 0)
    gate_end()

    scale_o[...] = jnp.transpose(scales[...])[: WIDTH // BLOCK, :]
    lax.fori_loop(ND - 1, ND, drain_rows, 0)
    lax.fori_loop(ND - 1, ND, drain_parts, 0)
    three = GS.at[pl.ds(0, NY - 1)]
    remote(three, three, gy_sem.at[0], gy_sem.at[1], ypeer(1)).wait_send()
    most = GO.at[pl.ds(0, NZ - 1)]
    remote(most, most, gz_sem.at[0], gz_sem.at[1], zpeer(1)).wait_send()


def per_device(cotangent, hidden, routes, numerators, w_down):
    whole = pl.BlockSpec(memory_space=pltpu.HBM)
    vmem = pl.BlockSpec(memory_space=pltpu.VMEM)
    dma = pltpu.SemaphoreType.DMA
    gate, scales, grad = pl.pallas_call(
        kernel,
        out_shape=(
            jax.ShapeDtypeStruct((TOP, TOK), F32),
            jax.ShapeDtypeStruct((WIDTH // BLOCK, SHARE), F32),
            jax.ShapeDtypeStruct((SHARE, WIDTH), F32),
        ),
        in_specs=[whole] * 5,
        out_specs=(vmem, vmem, vmem),
        scratch_shapes=[
            pltpu.VMEM((ND, NZ, TOK, DC), BF),
            pltpu.VMEM((NZ, PLANE, MAIN), BF),
            pltpu.VMEM((NZ, PLANE, MAIN), BF),
            pltpu.VMEM((NY, COLUMN, PADH), BF),
            pltpu.VMEM((NY * COLUMN, PADH), BF),
            pltpu.VMEM((PADH, ROUTED), BF),
            pltpu.VMEM((PADH, NY * COLUMN), BF),
            pltpu.VMEM((ND, PADH, DC), BF),
            pltpu.VMEM((2, NY * GROUP, HALF * TOK), BF),
            pltpu.VMEM((ND, NY, COLUMN, DC), BF),
            pltpu.VMEM((ND, NY, COLUMN, DC), BF),
            pltpu.VMEM((ND, NR, SHARE, DC), BF),
            pltpu.VMEM((ND, NR, SHARE, DC), BF),
            pltpu.VMEM((NY, COLUMN, BLOCK), F32),
            pltpu.VMEM((EXPERTS, TOK), F32),
            pltpu.VMEM((NY, NZ, BLOCK), F32),
            pltpu.VMEM((NY, NZ, BLOCK), F32),
            pltpu.VMEM((NZ, 8, BLOCK), F32),
            pltpu.VMEM((NZ, 8, BLOCK), F32),
            pltpu.VMEM((EXPERTS, BLOCK), F32),
            pltpu.VMEM((NY, COLUMN, DC), F32),
            pltpu.VMEM((SHARE, BLOCK), F32),
            pltpu.VMEM((NZ, LOW, BLOCK), BF),
            pltpu.VMEM((NZ, LOW, BLOCK), BF),
            pltpu.VMEM((HALF, PLANE, BLOCK), F32),
            pltpu.VMEM((TOP, TOK), jnp.int32),
            pltpu.VMEM((TOP, TOK), jnp.int32),
            dma((ND,)),
            dma((TOP,)),
            dma((ND,)),
            dma((7,)),
            dma((ND,)),
            dma((ND,)),
            dma((2, ND)),
            dma((2, ND, HALF)),
            dma((2,)),
            dma((2,)),
            dma((ND,)),
            dma((ND,)),
            dma((ND,)),
            dma((ND,)),
            dma((2,)),
            dma((2,)),
            dma((2,)),
        ],
        compiler_params=pltpu.CompilerParams(
            collective_id=0, has_side_effects=True, vmem_limit_bytes=52 * 1024 * 1024
        ),
    )(
        cotangent,
        hidden.transpose(1, 2, 0),
        routes.T,
        numerators.T,
        w_down[0],
    )
    return gate.T, scales.T[None], grad[None]


def solution(mesh):
    return jax.shard_map(
        per_device,
        mesh=mesh,
        in_specs=(
            P(("expert", "replica"), None),
            P(("expert", "replica"), None, None),
            P(("expert", "replica"), None),
            P(("expert", "replica"), None),
            P("expert", None, None),
        ),
        out_specs=(
            P(("expert", "replica"), None),
            P("expert", "replica", None),
            P("expert", "replica", None),
        ),
        check_vma=False,
    )
```

```python
import jax
import jax.numpy as jnp
from jax import lax
from jax.experimental import pallas as pl
from jax.experimental.pallas import tpu as pltpu
from jax.sharding import PartitionSpec as P

MESH = pl.DeviceIdType.MESH
BF, F32 = jnp.bfloat16, jnp.float32
BLOCK = 128
NZ, NY, NR = 16, 4, 8
EXPERTS = NZ * NY
SLOTS = 18
TOK, WIDTH, HID, TOP = 128, 2048, 704, 6
PADH = 768
MAIN = 640
LOW = 40
CODES = 3
HOME = 3
ROUTED = TOK * TOP
COLUMN = NZ * SLOTS
SHARE = HID // NR
DC = 256
ND = WIDTH // DC
HALF = NZ // 2
GROUP = HALF * SLOTS
PLANE = NY * SLOTS
STAGGER = 2
FULL = -(-HALF // STAGGER)
TURN = 1
NEAR = 2


def iota(shape, dim):
    return lax.broadcasted_iota(jnp.int32, shape, dim).astype(F32)


def one_where(condition):
    return jnp.where(condition, 1.0, 0.0).astype(BF)


def kernel(
    cot, hid6, routes_in, nums_in, w,
    gate_o, scale_o, grad_o,
    G, PK, HZ, YH, HY, hidL, hT, WS, SEL, YS, R, XS, XR, gacc, RK, GS, GM, GO, GR, G2, VS, scales, PT, TZ, ENDS, routes, nums,
    cot_sem, hid_sem, w_sem, own_sem, ylocal, xlocal,
    ring_send, ring_recv, hz_sem, hy_sem, ys_send, ys_recv, xs_send, xs_recv, gy_sem, gz_sem, ht_sem,
):
    expert = lax.axis_index("expert")
    rep = lax.axis_index("replica")
    z = lax.div(expert, NY)
    y = lax.rem(expert, NY)

    def zat(d):
        return lax.rem(z + d, NZ)

    def zpeer(d):
        return (zat(d) * NY + y, rep)

    def ypeer(d):
        return (z * NY + lax.rem(y + d, NY), rep)

    def xpeer(d):
        return (expert, lax.rem(rep + d, NR))

    def remote(src, dst, send, recv, peer):
        return pltpu.make_async_remote_copy(
            src_ref=src, dst_ref=dst, send_sem=send, recv_sem=recv,
            device_id=peer, device_id_type=MESH,
        )

    cot_loads = [
        pltpu.make_async_copy(cot.at[:, pl.ds(j * DC, DC)], G.at[j, HOME], cot_sem.at[j])
        for j in range(ND)
    ]
    hid_loads = [
        pltpu.make_async_copy(
            hid6.at[k], hidL.at[pl.ds(0, HID), pl.ds(k * TOK, TOK)], hid_sem.at[k]
        )
        for k in range(TOP)
    ]
    w_loads = [
        pltpu.make_async_copy(
            w.at[:, pl.ds(j * DC, DC)], WS.at[j, pl.ds(0, HID), :], w_sem.at[j]
        )
        for j in range(ND)
    ]
    small_loads = [
        pltpu.make_async_copy(routes_in, routes, own_sem.at[5]),
        pltpu.make_async_copy(nums_in, nums, own_sem.at[6]),
    ]
    for copy in small_loads + cot_loads + hid_loads + w_loads:
        copy.start()

    barrier = pltpu.get_barrier_semaphore()
    peers = (
        [zpeer(d) for d in range(1, NZ)]
        + [ypeer(d) for d in range(1, NY)]
        + [xpeer(d) for d in range(1, NR)]
    )
    for peer in peers:
        pl.semaphore_signal(barrier, inc=1, device_id=peer, device_id_type=MESH)
    pl.semaphore_wait(barrier, len(peers))

    def ring_copy(way, j, s):
        step = NZ - 1 if way == 0 else 1
        held, later = (HOME + step * s) % NZ, (HOME + step * (s + 1)) % NZ
        peer = zpeer(1) if way == 0 else zpeer(NZ - 1)
        return remote(
            G.at[j, held], G.at[j, later], ring_send.at[way, j], ring_recv.at[way, j, s], peer
        )

    def ring_arrival(way, j, s):
        ring_copy(way, j, s).wait_recv()

    for j in range(ND):
        cot_loads[j].wait()
        for way in range(2):
            ring_copy(way, j, 0).start()

    for copy in small_loads:
        copy.wait()
    which = iota((EXPERTS, TOK), 0)
    names = [routes[k : k + 1, :].astype(F32) for k in range(TOP)]
    member = jnp.zeros((EXPERTS, TOK), F32)
    for k in range(TOP):
        member = member + jnp.where(which == names[k], 1.0, 0.0)
    earlier = one_where(iota((TOK, TOK), 0) < iota((TOK, TOK), 1))
    before = jnp.dot(member.astype(BF), earlier, preferred_element_type=F32)
    RK[...] = jnp.where(member > 0.5, before, -1.0)
    slot_row = jnp.concatenate(
        [
            names[k] * float(SLOTS)
            + jnp.sum(jnp.where(which == names[k], before, 0.0), axis=0, keepdims=True)
            for k in range(TOP)
        ],
        axis=1,
    )
    n_row = jnp.concatenate([nums[k : k + 1, :].astype(F32) for k in range(TOP)], axis=1)
    n_high = jnp.floor(n_row * (1.0 / 32.0))
    n_low = n_row - 32.0 * n_high
    t_row = jnp.concatenate([iota((1, TOK), 1) + 1.0] * TOP, axis=1)
    extra_row = iota((PADH - HID, ROUTED), 0)
    extra = jnp.where(
        extra_row == 0.0,
        n_high,
        jnp.where(extra_row == 1.0, n_low, jnp.where(extra_row == 2.0, t_row, 0.0)),
    )
    hidL[HID:PADH, :] = extra.astype(BF)
    WS[:, HID:PADH, :] = jnp.zeros((ND, PADH - HID, DC), BF)
    GO[...] = jnp.zeros_like(GO)
    gacc[...] = jnp.zeros_like(gacc)
    for copy in hid_loads:
        copy.wait()

    def pack(i, carry):
        rows = iota((NY * PLANE, 1), 0) + (i * (NY * PLANE)).astype(F32)
        chosen = one_where(rows == slot_row)
        out = lax.dot_general(
            chosen, hidL[...], (((1,), (1,)), ((), ())), preferred_element_type=F32
        )
        PK[pl.ds(i * NY, NY)] = out[:, :MAIN].reshape(NY, PLANE, MAIN).astype(BF)
        ends = out[:, MAIN:].reshape(NY, PLANE, BLOCK)
        lane = iota((NY, 8, BLOCK), 2)
        codes = jnp.zeros((NY, 8, BLOCK), F32)
        for q in range(PLANE // 8):
            first = BLOCK // 2 + CODES * q
            moved = pltpu.roll(ends[:, 8 * q : 8 * q + 8, :], CODES * q, 2)
            here = jnp.logical_and(lane >= first, lane < first + CODES)
            codes = codes + jnp.where(here, moved, 0.0)
        for q in range(LOW // 8):
            low = ends[:, 8 * q : 8 * q + 8, :]
            if 8 * q + LOW < PLANE:
                start = 8 * q + LOW
                high = pltpu.roll(ends[:, start : start + 8, :], BLOCK // 2, 2)
            else:
                high = codes
            line = jnp.where(lane < BLOCK // 2, low, high)
            PT[pl.ds(i * NY, NY), 8 * q : 8 * q + 8, :] = line.astype(BF)
        return carry

    lax.fori_loop(0, NZ // NY, pack, 0)
    for d in (8, 7, 9, 6, 10, 5, 11, 4, 12, 3, 13, 2, 14, 1, 15):
        remote(PK.at[zat(d)], HZ.at[(HOME - d) % NZ], hz_sem.at[0], hz_sem.at[1], zpeer(d)).start()
        remote(PT.at[zat(d)], TZ.at[(HOME - d) % NZ], ht_sem.at[0], ht_sem.at[1], zpeer(d)).start()
    own_hz = pltpu.make_async_copy(PK.at[z], HZ.at[HOME], own_sem.at[0])
    own_hz.start()
    own_tz = pltpu.make_async_copy(PT.at[z], TZ.at[HOME], own_sem.at[4])
    own_tz.start()
    for copy in w_loads:
        copy.wait()

    def own_hy():
        return pltpu.make_async_copy(
            YH.at[y], HY.at[pl.ds(pl.multiple_of(y * COLUMN, COLUMN), COLUMN)], own_sem.at[1]
        )

    def hidden_mid():
        remote(
            HZ.at[pl.ds(0, NZ - 1)], HZ.at[pl.ds(0, NZ - 1)], hz_sem.at[0], hz_sem.at[1], zpeer(1)
        ).wait_recv()
        own_hz.wait()
        most = TZ.at[pl.ds(0, NZ - 1)]
        remote(most, most, ht_sem.at[0], ht_sem.at[1], zpeer(1)).wait_recv()
        own_tz.wait()
        out_row = iota((NY * GROUP, 1), 0)
        out_y = jnp.floor((out_row + 0.5) * (1.0 / GROUP))
        rest = out_row - out_y * GROUP
        out_z = jnp.floor((rest + 0.5) * (1.0 / SLOTS))
        out_r = rest - out_z * SLOTS
        source = out_z * PLANE + out_y * SLOTS + out_r
        permute = one_where(iota((NY * GROUP, NY * GROUP), 1) == source)
        for g in range(2):
            block = HZ[g * HALF : (g + 1) * HALF].astype(F32)
            lines = TZ[g * HALF : (g + 1) * HALF].astype(F32)
            lane = iota((HALF, 8, BLOCK), 2)
            for q in range(PLANE // 8):
                start = 8 * q if 8 * q < LOW else 8 * q - LOW
                values = lines[:, start : start + 8, :]
                if 8 * q >= LOW:
                    values = pltpu.roll(values, BLOCK // 2, 2)
                codes = pltpu.roll(lines[:, LOW - 8 : LOW, :], (BLOCK - CODES * q) % BLOCK, 2)
                kept = jnp.where(lane < BLOCK // 2 + CODES, codes, 0.0)
                ENDS[:, 8 * q : 8 * q + 8, :] = jnp.where(lane < BLOCK // 2, values, kept)
            main = block.reshape(HALF * PLANE, MAIN).astype(BF)
            ends = ENDS[...].reshape(HALF * PLANE, BLOCK).astype(BF)
            out = jnp.concatenate(
                [
                    jnp.dot(permute, main, preferred_element_type=F32),
                    jnp.dot(permute, ends, preferred_element_type=F32),
                ],
                axis=1,
            )
            token = out[:, HID + 2 : HID + 3]
            target = jnp.where(token > 0.5, token + out_z * TOK - 1.0, -1.0)
            SEL[g] = one_where(iota((NY * GROUP, HALF * TOK), 1) == target)
            rows = out.astype(BF)
            for yy in range(NY):
                YH[yy, g * GROUP : (g + 1) * GROUP, :] = rows[yy * GROUP : (yy + 1) * GROUP]
        mine = HY.at[pl.ds(pl.multiple_of(y * COLUMN, COLUMN), COLUMN)]
        for d in range(1, NY):
            remote(YH.at[lax.rem(y + d, NY)], mine, hy_sem.at[0], hy_sem.at[1], ypeer(d)).start()
        own_hy().start()

    def hidden_end():
        three = HY.at[pl.ds(0, (NY - 1) * COLUMN)]
        remote(three, three, hy_sem.at[0], hy_sem.at[1], ypeer(1)).wait_recv()
        own_hy().wait()

        def turn(i, carry):
            start = pl.multiple_of(i * TOK, TOK)
            rows = HY[pl.ds(start, TOK), :].astype(F32)
            weight = (rows[:, HID : HID + 1] * 32.0 + rows[:, HID + 1 : HID + 2]) * (1.0 / 1024.0)
            hT[:, pl.ds(start, TOK)] = jnp.transpose(rows * weight).astype(BF)
            return carry

        lax.fori_loop(0, NY * COLUMN // TOK, turn, 0)

    def drain_ring(c, carry):
        for way in range(2):
            sent = G.at[c, pl.ds(0, HALF - 1)]
            remote(sent, sent, ring_send.at[way, c], ring_recv.at[way, c, 0], zpeer(1)).wait_send()

            @pl.when(lax.rem(c + way, 2) == 1)
            def _(way=way):
                more = G.at[c, 0]
                remote(more, more, ring_send.at[way, c], ring_recv.at[way, c, 0], zpeer(1)).wait_send()

        return carry

    def drain_rows(c, carry):
        three = YS.at[c, pl.ds(0, NY - 1)]
        remote(three, three, ys_send.at[c], ys_recv.at[c], ypeer(1)).wait_send()
        return carry

    def drain_parts(c, carry):
        seven = XS.at[c, pl.ds(0, NR - 1)]
        remote(seven, seven, xs_send.at[c], xs_recv.at[c], xpeer(1)).wait_send()
        return carry

    def own_y(c):
        return pltpu.make_async_copy(YS.at[c, y], R.at[c, y], ylocal.at[c])

    def own_x(c):
        return pltpu.make_async_copy(XS.at[c, rep], XR.at[c, rep], xlocal.at[c])

    def select(c, g):
        if g == 1:
            for way in range(2):

                @pl.when(lax.rem(c + way, 2) == 1)
                def _(way=way):
                    ring_arrival(way, c, HALF - 1)
                    ring_arrival(1 - way, c, HALF - 2)

        block = G[c, g * HALF : (g + 1) * HALF].reshape(HALF * TOK, DC)
        out = jnp.dot(SEL[g], block, preferred_element_type=F32).astype(BF)
        rows = pl.ds(g * GROUP, GROUP)
        for yy in range(NY):
            YS[c, yy, g * GROUP : (g + 1) * GROUP, :] = out[yy * GROUP : (yy + 1) * GROUP]
        for d in range(1, NY):
            remote(
                YS.at[c, lax.rem(y + d, NY), rows],
                R.at[c, y, rows],
                ys_send.at[c],
                ys_recv.at[c],
                ypeer(d),
            ).start()
        if g == 1:
            own_y(c).start()

    def products(c):
        def ahead(b, carry):
            rows = HY[pl.ds(pl.multiple_of(b * COLUMN, COLUMN), COLUMN), :]
            VS[b] = jnp.dot(rows, WS[c], preferred_element_type=F32)
            return carry

        lax.fori_loop(0, NY, ahead, 0)

        @pl.when(c == ND - 1)
        def _():
            lax.fori_loop(0, ND, drain_ring, 0)
            lax.fori_loop(0, ND - 1, drain_rows, 0)
            most = PK.at[pl.ds(0, NZ - 1)]
            remote(most, most, hz_sem.at[0], hz_sem.at[1], zpeer(1)).wait_send()
            most = PT.at[pl.ds(0, NZ - 1)]
            remote(most, most, ht_sem.at[0], ht_sem.at[1], zpeer(1)).wait_send()
            half = YH.at[pl.ds(0, NY - 1)]
            remote(half, half, hy_sem.at[0], hy_sem.at[1], ypeer(1)).wait_send()

        three = R.at[c, pl.ds(0, NY - 1)]
        remote(three, three, ys_send.at[c], ys_recv.at[c], ypeer(1)).wait_recv()
        own_y(c).wait()

        def gates(b, carry):
            value = VS[b] * R[c, b].astype(F32)
            total = value[:, :BLOCK]
            for p in range(1, DC // BLOCK):
                total = total + value[:, p * BLOCK : (p + 1) * BLOCK]
            gacc[b] = gacc[b] + total
            return carry

        lax.fori_loop(0, NY, gates, 0)

        @pl.when(c == ND - 1)
        def _():
            gate_start()

        def part(i, carry):
            start = pl.multiple_of(i * (HID // 2), HID // 2)
            value = jnp.dot(
                hT[pl.ds(start, HID // 2), :],
                R[c].reshape(NY * COLUMN, DC),
                preferred_element_type=F32,
            )
            XS[c, pl.ds(i * (NR // 2), NR // 2)] = value.reshape(NR // 2, SHARE, DC).astype(BF)
            return carry

        lax.fori_loop(0, 2, part, 0)
        for d in range(1, NR):
            remote(
                XS.at[c, lax.rem(rep + d, NR)], XR.at[c, rep], xs_send.at[c], xs_recv.at[c], xpeer(d)
            ).start()
        own_x(c).start()

    def finish(c):
        seven = XR.at[c, pl.ds(0, NR - 1)]
        remote(seven, seven, xs_send.at[c], xs_recv.at[c], xpeer(1)).wait_recv()
        own_x(c).wait()
        first = XR[c, 0].astype(F32)
        total, largest = first, jnp.abs(first)
        for q in range(1, NR):
            value = XR[c, q].astype(F32)
            total = total + value
            largest = jnp.maximum(largest, jnp.abs(value))
        for p in range(DC // BLOCK):
            cols = slice(p * BLOCK, (p + 1) * BLOCK)
            scale = jnp.max(largest[:, cols], axis=1, keepdims=True) + 1e-6
            start = pl.multiple_of(c * DC + p * BLOCK, BLOCK)
            grad_o[:, pl.ds(start, BLOCK)] = total[:, cols] / scale
            number = (c * (DC // BLOCK) + p).astype(F32)
            scales[...] = jnp.where(iota((SHARE, BLOCK), 1) == number, scale, scales[...])

    scales[...] = jnp.zeros_like(scales)

    def own_gy():
        return pltpu.make_async_copy(GS.at[y], GM.at[y], own_sem.at[2])

    def own_gz():
        return pltpu.make_async_copy(GO.at[HOME], GR.at[z], own_sem.at[3])

    def gate_start():
        row = iota((COLUMN, BLOCK), 0)
        spread = row - SLOTS * jnp.floor((row + 0.5) * (1.0 / SLOTS)) == iota((COLUMN, BLOCK), 1)
        lane = iota((NZ, COLUMN), 1)
        gather = one_where(jnp.floor((lane + 0.5) * (1.0 / SLOTS)) == iota((NZ, COLUMN), 0))
        for yy in range(NY):
            column = jnp.sum(gacc[yy], axis=1, keepdims=True)
            value = jnp.where(spread, column, 0.0)
            total = jnp.zeros((NZ, BLOCK), F32)
            for _ in range(3):
                digit = value.astype(BF)
                total = total + jnp.dot(gather, digit, preferred_element_type=F32)
                value = value - digit.astype(F32)
            GS[yy] = total
        for d in range(1, NY):
            remote(GS.at[lax.rem(y + d, NY)], GM.at[y], gy_sem.at[0], gy_sem.at[1], ypeer(d)).start()
        own_gy().start()

    def gate_mid():
        three = GM.at[pl.ds(0, NY - 1)]
        remote(three, three, gy_sem.at[0], gy_sem.at[1], ypeer(1)).wait_recv()
        own_gy().wait()
        for yy in range(NY):
            for zz in range(NZ):
                GO[zz, yy : yy + 1, :] = GM[yy, zz : zz + 1, :]
        for d in range(1, NZ):
            remote(GO.at[(d + HOME) % NZ], GR.at[z], gz_sem.at[0], gz_sem.at[1], zpeer(d)).start()
        own_gz().start()

    def gate_end():
        most = GR.at[pl.ds(0, NZ - 1)]
        remote(most, most, gz_sem.at[0], gz_sem.at[1], zpeer(1)).wait_recv()
        own_gz().wait()
        for zz in range(NZ):
            G2[zz * NY : (zz + 1) * NY, :] = GR[zz, 0:NY, :]
        table = G2[...]
        ranks = RK[...]
        value = jnp.zeros((EXPERTS, TOK), F32)
        for s in range(SLOTS):
            value = value + jnp.where(ranks == float(s), table[:, s : s + 1], 0.0)
        for k in range(TOP):
            named = routes[k : k + 1, :].astype(F32)
            gate_o[k : k + 1, :] = jnp.sum(
                jnp.where(iota((EXPERTS, TOK), 0) == named, value, 0.0), axis=0, keepdims=True
            )

    last = HALF - 1

    def ring_steps(m, h):
        for s in range(last, 0, -1):
            if s % STAGGER != h:
                continue
            j = m - s // STAGGER
            valid = jnp.logical_and(j >= 0, j < ND)

            if s < last:

                @pl.when(valid)
                def _(s=s, j=j):
                    for way in range(2):
                        ring_arrival(way, j, s - 1)
                        ring_copy(way, j, s).start()

            else:
                for way in range(2):

                    @pl.when(jnp.logical_and(valid, lax.rem(j + way, 2) == 1))
                    def _(s=s, j=j, way=way):
                        ring_arrival(way, j, s - 1)
                        ring_copy(way, j, s).start()

    def body(m, carry):
        ring_steps(m, 0)

        @pl.when(jnp.logical_and(m >= FULL, m < ND + FULL))
        def _():
            select(m - FULL, 1)

        @pl.when(jnp.logical_and(m >= NEAR, m < ND + NEAR))
        def _():
            select(m - NEAR, 0)

        @pl.when(m == FULL)
        def _():
            hidden_end()

        for h in range(1, STAGGER):
            ring_steps(m, h)

        @pl.when(jnp.logical_and(m >= FULL + 1, m < ND + FULL + 1))
        def _():
            products(m - FULL - 1)

        @pl.when(m == TURN)
        def _():
            hidden_mid()

        @pl.when(m == ND + FULL + 1)
        def _():
            gate_mid()
            lax.fori_loop(0, ND - 1, drain_parts, 0)

        @pl.when(m >= FULL + 2)
        def _():
            finish(m - FULL - 2)

        return carry

    lax.fori_loop(0, ND + FULL + 2, body, 0)
    gate_end()

    scale_o[...] = jnp.transpose(scales[...])[: WIDTH // BLOCK, :]
    lax.fori_loop(ND - 1, ND, drain_rows, 0)
    lax.fori_loop(ND - 1, ND, drain_parts, 0)
    three = GS.at[pl.ds(0, NY - 1)]
    remote(three, three, gy_sem.at[0], gy_sem.at[1], ypeer(1)).wait_send()
    most = GO.at[pl.ds(0, NZ - 1)]
    remote(most, most, gz_sem.at[0], gz_sem.at[1], zpeer(1)).wait_send()


def per_device(cotangent, hidden, routes, numerators, w_down):
    whole = pl.BlockSpec(memory_space=pltpu.HBM)
    vmem = pl.BlockSpec(memory_space=pltpu.VMEM)
    dma = pltpu.SemaphoreType.DMA
    gate, scales, grad = pl.pallas_call(
        kernel,
        out_shape=(
            jax.ShapeDtypeStruct((TOP, TOK), F32),
            jax.ShapeDtypeStruct((WIDTH // BLOCK, SHARE), F32),
            jax.ShapeDtypeStruct((SHARE, WIDTH), F32),
        ),
        in_specs=[whole] * 5,
        out_specs=(vmem, vmem, vmem),
        scratch_shapes=[
            pltpu.VMEM((ND, NZ, TOK, DC), BF),
            pltpu.VMEM((NZ, PLANE, MAIN), BF),
            pltpu.VMEM((NZ, PLANE, MAIN), BF),
            pltpu.VMEM((NY, COLUMN, PADH), BF),
            pltpu.VMEM((NY * COLUMN, PADH), BF),
            pltpu.VMEM((PADH, ROUTED), BF),
            pltpu.VMEM((PADH, NY * COLUMN), BF),
            pltpu.VMEM((ND, PADH, DC), BF),
            pltpu.VMEM((2, NY * GROUP, HALF * TOK), BF),
            pltpu.VMEM((ND, NY, COLUMN, DC), BF),
            pltpu.VMEM((ND, NY, COLUMN, DC), BF),
            pltpu.VMEM((ND, NR, SHARE, DC), BF),
            pltpu.VMEM((ND, NR, SHARE, DC), BF),
            pltpu.VMEM((NY, COLUMN, BLOCK), F32),
            pltpu.VMEM((EXPERTS, TOK), F32),
            pltpu.VMEM((NY, NZ, BLOCK), F32),
            pltpu.VMEM((NY, NZ, BLOCK), F32),
            pltpu.VMEM((NZ, 8, BLOCK), F32),
            pltpu.VMEM((NZ, 8, BLOCK), F32),
            pltpu.VMEM((EXPERTS, BLOCK), F32),
            pltpu.VMEM((NY, COLUMN, DC), F32),
            pltpu.VMEM((SHARE, BLOCK), F32),
            pltpu.VMEM((NZ, LOW, BLOCK), BF),
            pltpu.VMEM((NZ, LOW, BLOCK), BF),
            pltpu.VMEM((HALF, PLANE, BLOCK), F32),
            pltpu.VMEM((TOP, TOK), jnp.int32),
            pltpu.VMEM((TOP, TOK), jnp.int32),
            dma((ND,)),
            dma((TOP,)),
            dma((ND,)),
            dma((7,)),
            dma((ND,)),
            dma((ND,)),
            dma((2, ND)),
            dma((2, ND, HALF)),
            dma((2,)),
            dma((2,)),
            dma((ND,)),
            dma((ND,)),
            dma((ND,)),
            dma((ND,)),
            dma((2,)),
            dma((2,)),
            dma((2,)),
        ],
        compiler_params=pltpu.CompilerParams(
            collective_id=0, has_side_effects=True, vmem_limit_bytes=52 * 1024 * 1024
        ),
    )(
        *(
            pltpu.with_memory_space_constraint(value, pltpu.HBM)
            for value in (
                cotangent,
                hidden.transpose(1, 2, 0),
                routes.T,
                numerators.T,
                w_down[0],
            )
        )
    )
    return gate.T, scales.T[None], grad[None]


def solution(mesh):
    return jax.shard_map(
        per_device,
        mesh=mesh,
        in_specs=(
            P(("expert", "replica"), None),
            P(("expert", "replica"), None, None),
            P(("expert", "replica"), None),
            P(("expert", "replica"), None),
            P("expert", None, None),
        ),
        out_specs=(
            P(("expert", "replica"), None),
            P("expert", "replica", None),
            P("expert", "replica", None),
        ),
        check_vma=False,
    )
```
